32 devices in a mesh: sp: 8 (over z, core), fsdp: 4 (over y, x).
Axes of the slice: x: 2, y: 2, z: 4, core: 2. Of those that a mesh axis runs over, the one named last changes fastest.
Arguments:
- hidden_in: bfloat16 [4, 2048, 1024], P('fsdp', 'sp'), may hold values from -6 to 6
- positions: int32 [4, 2048], P('fsdp', 'sp'), may hold values from 0 to 2047, as said below
- out_cotangent: bfloat16 [4, 2048, 1024], P('fsdp', 'sp'), may hold values from -6 to 6
- attn_gain: bfloat16 [1024], P('fsdp'), may hold values from 0.099609375 to 1.8984375
- attn_shift: bfloat16 [1024], P('fsdp'), may hold values from -3 to 3
- mlp_gain: bfloat16 [1024], P('fsdp'), may hold values from 0.099609375 to 1.8984375
- mlp_shift: bfloat16 [1024], P('fsdp'), may hold values from -3 to 3
- qkv_weight: bfloat16 [1024, 3072], P('fsdp')
- qkv_bias: bfloat16 [3072], P('fsdp'), may hold values from -3 to 3
- dense_weight: bfloat16 [1024, 1024], P('fsdp'), may hold values from -1.5 to 1.5
- dense_bias: bfloat16 [1024], P('fsdp'), may hold values from -3 to 3
- up_weight: bfloat16 [1024, 4096], P('fsdp'), may hold values from -0.1875 to 0.1875
- up_bias: bfloat16 [4096], P('fsdp'), may hold values from -3 to 3
- down_weight: bfloat16 [4096, 1024], P('fsdp'), may hold values from -0.09375 to 0.09375
- down_bias: bfloat16 [1024], P('fsdp'), may hold values from -3 to 3
Outputs:
- block_out: bfloat16 [4, 2048, 1024], P('fsdp', 'sp')
- input_grad: float32 [4, 2048, 1024], P('fsdp', 'sp')
- attn_gain_grad: float32 [1024], P(('sp', 'fsdp'))
- attn_shift_grad: float32 [1024], P(('sp', 'fsdp'))
- mlp_gain_grad: float32 [1024], P(('sp', 'fsdp'))
- mlp_shift_grad: float32 [1024], P(('sp', 'fsdp'))
- qkv_weight_grad: float32 [1024, 3072], P(('sp', 'fsdp'))
- qkv_bias_grad: float32 [3072], P(('sp', 'fsdp'))
- dense_weight_grad: float32 [1024, 1024], P(('sp', 'fsdp'))
- dense_bias_grad: float32 [1024], P(('sp', 'fsdp'))
- up_weight_grad: float32 [1024, 4096], P(('sp', 'fsdp'))
- up_bias_grad: float32 [4096], P(('sp', 'fsdp'))
- down_weight_grad: float32 [4096, 1024], P(('sp', 'fsdp'))
- down_bias_grad: float32 [1024], P(('sp', 'fsdp'))
The draws below stay inside these ranges and needn't reach their ends.
Inputs may be any that keep to these rules, and one draw needn't show every extreme that they name: Each sequence is a pack of whole documents: a token's position is its distance to its document's first token, so positions are 0 where a document begins and rise by one per token inside a document; every sequence begins a document.
All inputs are finite; a program needn't handle non-finite values.
Results may differ from the reference program's by a relative error of at most 0.011.
Values may be sent and summed in bfloat16 or wider, within the bound.
A program may use at most 256 MiB of HBM per device.

```python
import math
import jax
import jax.numpy as jnp
from jax import lax

D = 1024
HEADS = 16
HD = 64
ROT = 16
FF = 4096
SEQ_LEN = 2048
SEQS_ALL = 4


def draw_qkv_weight(key, part):
    weights_all = jax.random.normal(jax.random.fold_in(key, 11), (D, HEADS, 3, HD), jnp.float32) * D ** (-0.5)
    return weights_all.reshape(D, 3 * D).astype(jnp.bfloat16)


def draw_positions(key, part):
    grid_shape = (SEQS_ALL, SEQ_LEN)
    breaks = jax.random.randint(jax.random.fold_in(key, 21), grid_shape, 0, SEQ_LEN) < 4
    column = jnp.arange(SEQ_LEN, dtype=jnp.int32)[None, :]
    first_row = jnp.arange(SEQS_ALL, dtype=jnp.int32)[:, None] == 0
    breaks = breaks & jnp.logical_not(first_row) | (column == 0)
    starts = lax.cummax(jnp.where(breaks, column, 0), axis=1)
    return (column - starts).astype(jnp.int32)


def shard_levels(rng, dims, shards, least, top_value):
    def one(axis_at, blocks):
        steps = jax.random.uniform(jax.random.fold_in(jax.random.fold_in(rng, 6), axis_at), (blocks,), jnp.float32, least / len(shards), top_value / len(shards))
        return jnp.repeat(jnp.exp(steps), dims[axis_at] // blocks).reshape((-1,) + (1,) * (len(dims) - axis_at - 1))

    loudness = one(*shards[0])
    for cut in shards[1:]:
        loudness = loudness * one(*cut)
    return loudness


def noise(key, extent, deviation, bound, cuts=(), held_as=jnp.bfloat16):
    drawn = jax.random.normal(key, extent, jnp.float32) * deviation
    if len(cuts) > 0:
        drawn = shard_levels(key, extent, cuts, -0.22, 0.18) * drawn
    return jnp.clip(drawn, min=-bound, max=bound).astype(held_as)


def setup_inputs(seed: int = 0) -> dict:
    arg_keys = jax.random.split(jax.random.key(seed), 16)
    hidden_in = noise(arg_keys[0], (SEQS_ALL, SEQ_LEN, D), 1.0, 6.0, ((0, 4), (1, 8)))
    positions = draw_positions(jax.random.fold_in(arg_keys[15], 71), 0)
    out_cotangent = noise(arg_keys[2], (SEQS_ALL, SEQ_LEN, D), 1.0, 6.0, ((0, 4), (1, 8)))
    attn_gain = jnp.clip(1.0 + 0.18 * jax.random.normal(arg_keys[3], (D,), jnp.float32), 0.099609375, 1.8984375).astype(jnp.bfloat16)
    attn_shift = noise(arg_keys[4], (D,), 0.5, 3.0, ((0, 4),))
    mlp_gain = jnp.clip(1.0 + 0.18 * jax.random.normal(arg_keys[5], (D,), jnp.float32), 0.099609375, 1.8984375).astype(jnp.bfloat16)
    mlp_shift = noise(arg_keys[6], (D,), 0.5, 3.0, ((0, 4),))
    qkv_weight = draw_qkv_weight(jax.random.fold_in(arg_keys[15], 71), 0)
    qkv_bias = noise(arg_keys[8], (3 * D,), 0.5, 3.0, ((0, 4),))
    dense_weight = noise(arg_keys[9], (D, D), (D // 64) ** -0.5, 1.5, ((0, 4),))
    dense_bias = noise(arg_keys[10], (D,), 0.5, 3.0, ((0, 4),))
    up_weight = noise(arg_keys[11], (D, FF), D ** -0.5, 0.1875, ((0, 4),))
    up_bias = noise(arg_keys[12], (FF,), 0.5, 3.0, ((0, 4),))
    down_weight = noise(arg_keys[13], (FF, D), FF ** -0.5, 0.09375, ((0, 4),))
    down_bias = noise(arg_keys[14], (D,), 0.5, 3.0, ((0, 4),))
    return {"hidden_in": hidden_in, "positions": positions, "out_cotangent": out_cotangent, "attn_gain": attn_gain, "attn_shift": attn_shift, "mlp_gain": mlp_gain, "mlp_shift": mlp_shift, "qkv_weight": qkv_weight, "qkv_bias": qkv_bias, "dense_weight": dense_weight, "dense_bias": dense_bias, "up_weight": up_weight, "up_bias": up_bias, "down_weight": down_weight, "down_bias": down_bias}


NORM_EPS = 1e-05
ROPE_BASE = 10000.0
ROOT_HALF = 0.7071067811865476
INV_ROOT_TWO_PI = 0.3989422804014327
MASK_FILL = -1e+30

def layer_norm(values):
    row_mean = lax.optimization_barrier(jnp.mean(values, axis=-1, keepdims=True))
    centered = values - row_mean
    inv_std = lax.rsqrt(lax.optimization_barrier(jnp.mean(centered * centered, axis=-1, keepdims=True)) + NORM_EPS)
    return (centered * inv_std, inv_std)

def affine(normed, norm_gain, norm_shift):
    return normed * norm_gain.astype(jnp.float32) + norm_shift.astype(jnp.float32)

def norm_backward(grad_out, normed, inv_std, norm_gain):
    grad_normed = grad_out * norm_gain.astype(jnp.float32)
    mean_grad = lax.optimization_barrier(jnp.mean(grad_normed, axis=-1, keepdims=True))
    mean_cross = lax.optimization_barrier(jnp.mean(grad_normed * normed, axis=-1, keepdims=True))
    return inv_std * (grad_normed - mean_grad - normed * mean_cross)

def gelu_pair(hidden):
    cdf_part = 0.5 * (1.0 + jax.scipy.special.erf(hidden * ROOT_HALF))
    density = jnp.exp(-0.5 * hidden * hidden) * INV_ROOT_TWO_PI
    return (hidden * cdf_part, cdf_part + hidden * density)

def rope_tables(positions, rot_dims):
    half_dims = rot_dims // 2
    inv_freq = jnp.exp(jnp.arange(half_dims, dtype=jnp.float32) * (-2.0 * math.log(ROPE_BASE) / rot_dims))
    angles = positions.astype(jnp.float32)[..., None] * inv_freq
    angles = jnp.concatenate([angles, angles], axis=-1)
    return (jnp.cos(angles), jnp.sin(angles))

def rotate(values, cosine, sine_table, rot_dims):
    half_dims = rot_dims // 2
    leading = values[..., :rot_dims]
    turned = jnp.concatenate([-leading[..., half_dims:], leading[..., :half_dims]], axis=-1)
    leading = leading * cosine[..., None, :] + turned * sine_table[..., None, :]
    return jnp.concatenate([leading, values[..., rot_dims:]], axis=-1)

def rotate_back(grad_values, cosine, sine_table, rot_dims):
    half_dims = rot_dims // 2
    leading = grad_values[..., :rot_dims]
    scaled = leading * sine_table[..., None, :]
    leading = leading * cosine[..., None, :] + jnp.concatenate([scaled[..., half_dims:], -scaled[..., :half_dims]], axis=-1)
    return jnp.concatenate([leading, grad_values[..., rot_dims:]], axis=-1)

def reference(hidden_in, positions, out_cotangent, attn_gain, attn_shift, mlp_gain, mlp_shift, qkv_weight, qkv_bias, dense_weight, dense_bias, up_weight, up_bias, down_weight, down_bias):
    scale_value = 1.0 / math.sqrt(HD)
    length = SEQ_LEN

    def one_sequence(running, inputs):
        tokens_seq, pos_seq, cot_seq = inputs
        x_full = tokens_seq.astype(jnp.float32)
        normed, inv_std = layer_norm(x_full)
        attn_in = affine(normed, attn_gain, attn_shift).astype(jnp.bfloat16)
        mlp_in = affine(normed, mlp_gain, mlp_shift).astype(jnp.bfloat16)
        joined = jnp.dot(attn_in, qkv_weight, preferred_element_type=jnp.float32) + qkv_bias.astype(jnp.float32)
        joined = joined.reshape(length, HEADS, 3, HD)
        cosine, sine_table = rope_tables(pos_seq, ROT)
        query_all = rotate(joined[:, :, 0], cosine, sine_table, ROT).astype(jnp.bfloat16).transpose(1, 0, 2)
        key_all = rotate(joined[:, :, 1], cosine, sine_table, ROT).astype(jnp.bfloat16).transpose(1, 0, 2)
        value_all = joined[:, :, 2].astype(jnp.bfloat16).transpose(1, 0, 2)
        row_index = jnp.arange(length, dtype=jnp.int32)
        doc_start = row_index - pos_seq.astype(jnp.int32)
        allowed = (row_index[None, :] <= row_index[:, None]) & (row_index[None, :] >= doc_start[:, None])

        def masked_scores(query_rows, key_rows):
            scores = jnp.dot(query_rows, key_rows.T, preferred_element_type=jnp.float32) * scale_value
            return jnp.where(allowed, scores, MASK_FILL)

        def head_forward(operands):
            query_rows, key_rows, value_rows = operands
            scores = masked_scores(query_rows, key_rows)
            row_max = lax.optimization_barrier(jnp.max(scores, axis=-1, keepdims=True))
            log_total = row_max + jnp.log(lax.optimization_barrier(jnp.sum(jnp.exp(scores - row_max), axis=-1, keepdims=True)))
            attn_probs = jnp.exp(scores - log_total).astype(jnp.bfloat16)
            mixed = jnp.dot(attn_probs, value_rows, preferred_element_type=jnp.float32).astype(jnp.bfloat16)
            return (mixed, log_total[:, 0])

        def head_backward(operands):
            query_rows, key_rows, value_rows, grad_heads, log_total = operands
            scores = masked_scores(query_rows, key_rows)
            probs_full = jnp.exp(scores - log_total[:, None])
            probs_half = probs_full.astype(jnp.bfloat16)
            grad_probs = jnp.dot(grad_heads, value_rows.T, preferred_element_type=jnp.float32)
            row_delta = lax.optimization_barrier(jnp.sum(probs_full * grad_probs, axis=-1, keepdims=True))
            grad_scores = (scale_value * probs_full * (grad_probs - row_delta)).astype(jnp.bfloat16)
            grad_query = jnp.dot(grad_scores, key_rows, preferred_element_type=jnp.float32)
            grad_key = jnp.dot(grad_scores.T, query_rows, preferred_element_type=jnp.float32)
            grad_value = jnp.dot(probs_half.T, grad_heads, preferred_element_type=jnp.float32)
            return (grad_query, grad_key, grad_value)
        mixed_heads, log_totals = lax.map(head_forward, (query_all, key_all, value_all))
        mixed_rows = mixed_heads.transpose(1, 0, 2).reshape(length, D)
        attn_out = jnp.dot(mixed_rows, dense_weight, preferred_element_type=jnp.float32) + dense_bias.astype(jnp.float32)
        up_out = jnp.dot(mlp_in, up_weight, preferred_element_type=jnp.float32) + up_bias.astype(jnp.float32)
        activated, gelu_slope = gelu_pair(up_out)
        activated = activated.astype(jnp.bfloat16)
        mlp_out = jnp.dot(activated, down_weight, preferred_element_type=jnp.float32) + down_bias.astype(jnp.float32)
        block_seq = (x_full + attn_out + mlp_out).astype(jnp.bfloat16)
        grad_full = cot_seq.astype(jnp.float32)
        grad_down = jnp.dot(activated.T, cot_seq, preferred_element_type=jnp.float32)
        output_bias_grad = lax.optimization_barrier(jnp.sum(grad_full, axis=0))
        grad_up = jnp.dot(cot_seq, down_weight.T, preferred_element_type=jnp.float32) * gelu_slope
        grad_up_half = grad_up.astype(jnp.bfloat16)
        grad_up_weight = jnp.dot(mlp_in.T, grad_up_half, preferred_element_type=jnp.float32)
        up_bias_grad = lax.optimization_barrier(jnp.sum(grad_up, axis=0))
        grad_mlp_in = jnp.dot(grad_up_half, up_weight.T, preferred_element_type=jnp.float32)
        grad_dense = jnp.dot(mixed_rows.T, cot_seq, preferred_element_type=jnp.float32)
        grad_mixed = jnp.dot(cot_seq, dense_weight.T, preferred_element_type=jnp.float32).astype(jnp.bfloat16)
        grad_mixed = grad_mixed.reshape(length, HEADS, HD).transpose(1, 0, 2)
        grad_query, grad_key, grad_value = lax.map(head_backward, (query_all, key_all, value_all, grad_mixed, log_totals))
        sent_query, sent_key, sent_value = lax.optimization_barrier((grad_query.astype(jnp.bfloat16), grad_key.astype(jnp.bfloat16), grad_value.astype(jnp.bfloat16)))
        sent_query = sent_query.transpose(1, 0, 2).astype(jnp.float32)
        sent_key = sent_key.transpose(1, 0, 2).astype(jnp.float32)
        sent_value = sent_value.transpose(1, 0, 2).astype(jnp.float32)
        grad_joined = jnp.stack([rotate_back(sent_query, cosine, sine_table, ROT), rotate_back(sent_key, cosine, sine_table, ROT), sent_value], axis=2).reshape(length, 3 * D)
        qkv_bias_grad = lax.optimization_barrier(jnp.sum(grad_joined, axis=0))
        grad_joined_half = grad_joined.astype(jnp.bfloat16)
        grad_qkv = jnp.dot(attn_in.T, grad_joined_half, preferred_element_type=jnp.float32)
        grad_attn_in = jnp.dot(grad_joined_half, qkv_weight.T, preferred_element_type=jnp.float32)
        attn_gain_grad = lax.optimization_barrier(jnp.sum(grad_attn_in * normed, axis=0))
        attn_shift_grad = lax.optimization_barrier(jnp.sum(grad_attn_in, axis=0))
        mlp_gain_grad = lax.optimization_barrier(jnp.sum(grad_mlp_in * normed, axis=0))
        mlp_shift_grad = lax.optimization_barrier(jnp.sum(grad_mlp_in, axis=0))
        grad_input = grad_full + norm_backward(grad_attn_in, normed, inv_std, attn_gain) + norm_backward(grad_mlp_in, normed, inv_std, mlp_gain)
        terms = (attn_gain_grad, attn_shift_grad, mlp_gain_grad, mlp_shift_grad, grad_qkv, qkv_bias_grad, grad_dense, output_bias_grad, grad_up_weight, up_bias_grad, grad_down)
        running = tuple((total + term for total, term in zip(running, terms)))
        return (running, (block_seq, grad_input))
    start_totals = (jnp.zeros((D,), jnp.float32), jnp.zeros((D,), jnp.float32), jnp.zeros((D,), jnp.float32), jnp.zeros((D,), jnp.float32), jnp.zeros((D, 3 * D), jnp.float32), jnp.zeros((3 * D,), jnp.float32), jnp.zeros((D, D), jnp.float32), jnp.zeros((D,), jnp.float32), jnp.zeros((D, FF), jnp.float32), jnp.zeros((FF,), jnp.float32), jnp.zeros((FF, D), jnp.float32))
    totals, (block_out, input_grad) = lax.scan(one_sequence, start_totals, (hidden_in, positions, out_cotangent))
    return (block_out, input_grad, totals[0], totals[1], totals[2], totals[3], totals[4], totals[5], totals[6], totals[7], totals[8], totals[9], totals[10], totals[7])
```

```python
import functools
import math

import jax
import jax.numpy as jnp
from jax import lax
from jax.experimental import pallas as pl
from jax.experimental.pallas import tpu as pltpu
from jax.sharding import PartitionSpec as P

HEADS = 16
HD = 64
ROT = 16


NORM_EPS = 1e-05
ROPE_BASE = 10000.0
ROOT_HALF = 0.7071067811865476
INV_ROOT_TWO_PI = 0.3989422804014327
MASK_FILL = -1e30


def layer_norm(values):
    row_mean = jnp.mean(values, axis=-1, keepdims=True)
    centered = values - row_mean
    inv_std = lax.rsqrt(jnp.mean(centered * centered, axis=-1, keepdims=True) + NORM_EPS)
    return (centered * inv_std, inv_std)


def affine(normed, norm_gain, norm_shift):
    return normed * norm_gain.astype(jnp.float32) + norm_shift.astype(jnp.float32)


def norm_backward(grad_out, normed, inv_std, norm_gain):
    grad_normed = grad_out * norm_gain.astype(jnp.float32)
    mean_grad = jnp.mean(grad_normed, axis=-1, keepdims=True)
    mean_cross = jnp.mean(grad_normed * normed, axis=-1, keepdims=True)
    return inv_std * (grad_normed - mean_grad - normed * mean_cross)


def gelu_pair(hidden):
    cdf_part = 0.5 * (1.0 + jax.scipy.special.erf(hidden * ROOT_HALF))
    density = jnp.exp(-0.5 * hidden * hidden) * INV_ROOT_TWO_PI
    return (hidden * cdf_part, cdf_part + hidden * density)


def rope_tables(positions, rot_dims):
    half_dims = rot_dims // 2
    inv_freq = jnp.exp(
        jnp.arange(half_dims, dtype=jnp.float32) * (-2.0 * math.log(ROPE_BASE) / rot_dims)
    )
    angles = positions.astype(jnp.float32)[..., None] * inv_freq
    angles = jnp.concatenate([angles, angles], axis=-1)
    return (jnp.cos(angles), jnp.sin(angles))


def rotate(values, cosine, sine_table, rot_dims):
    half_dims = rot_dims // 2
    leading = values[..., :rot_dims]
    turned = jnp.concatenate([-leading[..., half_dims:], leading[..., :half_dims]], axis=-1)
    leading = leading * cosine[..., None, :] + turned * sine_table[..., None, :]
    return jnp.concatenate([leading, values[..., rot_dims:]], axis=-1)


def rotate_back(grad_values, cosine, sine_table, rot_dims):
    half_dims = rot_dims // 2
    leading = grad_values[..., :rot_dims]
    scaled = leading * sine_table[..., None, :]
    leading = leading * cosine[..., None, :] + jnp.concatenate(
        [scaled[..., half_dims:], -scaled[..., :half_dims]], axis=-1
    )
    return jnp.concatenate([leading, grad_values[..., rot_dims:]], axis=-1)


def allowed_block(all_positions, row_start, block_rows, key_len):
    row_index = row_start + jnp.arange(block_rows, dtype=jnp.int32)
    col_index = jnp.arange(key_len, dtype=jnp.int32)
    doc_start = row_index[None, :] - all_positions[:, row_start : row_start + block_rows]
    allowed = (col_index[None, None, :] <= row_index[None, :, None]) & (
        col_index[None, None, :] >= doc_start[:, :, None]
    )
    return allowed[:, None]


def block_scores(
    query_block, key_part, all_positions, row_start, block_rows, row_stop, scale_value
):
    scores = (
        jnp.einsum("sqhd,skhd->shqk", query_block, key_part, preferred_element_type=jnp.float32)
        * scale_value
    )
    return jnp.where(
        allowed_block(all_positions, row_start, block_rows, row_stop), scores, MASK_FILL
    )


def attend_forward(head_side, all_positions):
    seq_count, length, heads_here, packed_width = head_side.shape
    head_dim = packed_width // 3
    query_rows = head_side[..., :head_dim]
    key_rows = head_side[..., head_dim : 2 * head_dim]
    value_rows = head_side[..., 2 * head_dim :]
    block_rows = min(512, length)
    scale_value = 1.0 / math.sqrt(head_dim)
    outputs = []
    totals = []
    for block_index in range(length // block_rows):
        row_start = block_index * block_rows
        row_stop = row_start + block_rows
        scores = block_scores(
            query_rows[:, row_start:row_stop],
            key_rows[:, :row_stop],
            all_positions,
            row_start,
            block_rows,
            row_stop,
            scale_value,
        )
        row_max = jnp.max(scores, axis=-1, keepdims=True)
        log_total = row_max + jnp.log(jnp.sum(jnp.exp(scores - row_max), axis=-1, keepdims=True))
        attn_probs = jnp.exp(scores - log_total).astype(jnp.bfloat16)
        outputs.append(
            jnp.einsum(
                "shqk,skhd->sqhd",
                attn_probs,
                value_rows[:, :row_stop],
                preferred_element_type=jnp.float32,
            ).astype(jnp.bfloat16)
        )
        totals.append(log_total)
    return (jnp.concatenate(outputs, axis=1), jnp.concatenate(totals, axis=2))


def attend_backward(head_side, all_positions, grad_heads, log_total):
    seq_count, length, heads_here, packed_width = head_side.shape
    head_dim = packed_width // 3
    query_rows = head_side[..., :head_dim]
    key_rows = head_side[..., head_dim : 2 * head_dim]
    value_rows = head_side[..., 2 * head_dim :]
    block_rows = min(512, length)
    scale_value = 1.0 / math.sqrt(head_dim)
    query_parts = []
    grad_key_sum = jnp.zeros((seq_count, length, heads_here, head_dim), jnp.float32)
    grad_value_sum = jnp.zeros((seq_count, length, heads_here, head_dim), jnp.float32)
    for block_index in range(length // block_rows):
        row_start = block_index * block_rows
        row_stop = row_start + block_rows
        query_block = query_rows[:, row_start:row_stop]
        key_part = key_rows[:, :row_stop]
        value_part = value_rows[:, :row_stop]
        grad_block = grad_heads[:, row_start:row_stop]
        scores = block_scores(
            query_block, key_part, all_positions, row_start, block_rows, row_stop, scale_value
        )
        probs_full = jnp.exp(scores - log_total[:, :, row_start:row_stop])
        probs_half = probs_full.astype(jnp.bfloat16)
        grad_probs = jnp.einsum(
            "sqhd,skhd->shqk", grad_block, value_part, preferred_element_type=jnp.float32
        )
        row_delta = jnp.sum(probs_full * grad_probs, axis=-1, keepdims=True)
        grad_scores = (scale_value * probs_full * (grad_probs - row_delta)).astype(jnp.bfloat16)
        query_parts.append(
            jnp.einsum("shqk,skhd->sqhd", grad_scores, key_part, preferred_element_type=jnp.float32)
        )
        grad_key_sum = grad_key_sum.at[:, :row_stop].add(
            jnp.einsum(
                "shqk,sqhd->skhd", grad_scores, query_block, preferred_element_type=jnp.float32
            )
        )
        grad_value_sum = grad_value_sum.at[:, :row_stop].add(
            jnp.einsum(
                "shqk,sqhd->skhd", probs_half, grad_block, preferred_element_type=jnp.float32
            )
        )
    grad_query = jnp.concatenate(query_parts, axis=1)
    return jnp.concatenate([grad_query, grad_key_sum, grad_value_sum], axis=-1).astype(jnp.bfloat16)


MESH = pl.DeviceIdType.MESH


def remote(src, dst, send_sem, recv_sem, **target):
    return pltpu.make_async_remote_copy(
        src_ref=src, dst_ref=dst, send_sem=send_sem, recv_sem=recv_sem,
        device_id=target, device_id_type=MESH,
    )


def entry_barrier(targets):
    barrier = pltpu.get_barrier_semaphore()
    for target in targets:
        pl.semaphore_signal(barrier, inc=1, device_id=target, device_id_type=MESH)
    pl.semaphore_wait(barrier, len(targets))


def gather_kernel(
    sp, fsdp,
    x_ref, pos_ref, vec_ref, qkv_ref, up_ref, down_ref, dense_ref,
    x_out, pos_out, vec_out, qkv_out, up_out, down_out, dense_out,
    own_sem, line_send, x_recv, pos_send, pos_recv, w_send, w_recv,
):
    s, f = lax.axis_index("sp"), lax.axis_index("fsdp")
    chips = sp // 2
    chip, core = s // 2, s % 2
    partner = chip * 2 + (1 - core)
    head_rows = dense_out.shape[0]
    ff_piece = down_out.shape[1]
    dense_owner = s // (sp // fsdp)
    dense_part = s % (sp // fsdp)
    dense_src = dense_ref.at[pl.ds(pl.multiple_of(dense_part * head_rows, head_rows), head_rows)]
    down_src = down_ref.at[pl.ds(pl.multiple_of(s * ff_piece, ff_piece), ff_piece)]
    has_right, has_left = chip < chips - 1, chip > 0

    entry_barrier(
        [{"sp": (s + d) % sp} for d in range(1, sp)]
        + [{"fsdp": (f + d) % fsdp} for d in range(1, fsdp)]
    )

    def x_copy(src, block, sem, target):
        return remote(src, x_out.at[block], sem, x_recv.at[block], sp=target)

    def on(cond, copy, action):
        @pl.when(cond)
        def _():
            getattr(copy, action)()

    right = [x_copy(x_ref, s, line_send.at[0, 0], s + 2)]
    left = [x_copy(x_ref, s, line_send.at[1, 0], s - 2)]
    across_left = [x_copy(x_ref, s, line_send.at[2, 0], partner)]
    across_right = [None]
    on(has_right, right[0], "start")
    on(has_left, left[0], "start")
    across_left[0].start()

    pieces = [(vec_ref, vec_out), (qkv_ref, qkv_out), (up_ref, up_out), (down_src, down_out)]
    sends = []
    for d in range(1, fsdp):
        peer = (f + d) % fsdp
        for k, (src, out) in enumerate(pieces[:2]):
            sends.append(remote(src, out.at[f], w_send.at[k, d], w_recv.at[k, f], fsdp=peer))
    dense_sends = [
        remote(dense_src, dense_out, w_send.at[4, d], w_recv.at[4, 0], fsdp=(f + d) % fsdp)
        for d in range(1, fsdp)
    ]
    for d in range(1, fsdp):
        peer = (f + d) % fsdp
        for k, (src, out) in enumerate(pieces[2:]):
            sends.append(
                remote(src, out.at[f], w_send.at[k + 2, d], w_recv.at[k + 2, f], fsdp=peer)
            )
    for copy in sends[: 2 * (fsdp - 1)]:
        copy.start()
    is_owner = f == dense_owner
    for copy in dense_sends:
        on(is_owner, copy, "start")
    for copy in sends[2 * (fsdp - 1) :]:
        copy.start()
    pos_sends = []
    for d in range(1, sp):
        peer = (s + d) % sp
        pos_sends.append(remote(pos_ref, pos_out.at[s], pos_send.at[d], pos_recv.at[s], sp=peer))
        pos_sends[-1].start()
    own = [
        pltpu.make_async_copy(src, out.at[f], own_sem.at[k])
        for k, (src, out) in enumerate(pieces)
    ]
    own.append(pltpu.make_async_copy(x_ref, x_out.at[s], own_sem.at[4]))
    own.append(pltpu.make_async_copy(pos_ref, pos_out.at[s], own_sem.at[5]))
    own_dense = pltpu.make_async_copy(dense_src, dense_out, own_sem.at[6])
    for copy in own:
        copy.start()
    on(is_owner, own_dense, "start")

    for k in range(1, chips):
        from_left, from_right = s - 2 * k, s + 2 * k
        has_l, has_r = chip >= k, chip + k <= chips - 1
        held_l, held_r = x_out.at[from_left], x_out.at[from_right]
        right.append(x_copy(held_l, from_left, line_send.at[0, k], s + 2))
        left.append(x_copy(held_r, from_right, line_send.at[1, k], s - 2))
        across_left.append(x_copy(held_l, from_left, line_send.at[2, k], partner))
        across_right.append(x_copy(held_r, from_right, line_send.at[3, k], partner))

        @pl.when(has_l)
        def _():
            across_left[k].wait_recv()

            @pl.when(has_right)
            def _():
                right[k].start()

            across_left[k].start()

        @pl.when(has_r)
        def _():
            across_right[k].wait_recv()

            @pl.when(has_left)
            def _():
                left[k].start()

            across_right[k].start()

    for c in range(chips):
        block = 2 * c + (1 - core)
        x_copy(x_ref, block, line_send.at[0, 0], partner).wait_recv()
    for d in range(1, sp):
        block = (s + d) % sp
        remote(pos_ref, pos_out.at[block], pos_send.at[0], pos_recv.at[block], sp=block).wait_recv()
    for d in range(1, fsdp):
        peer = (f + d) % fsdp
        for k, (src, out) in enumerate(pieces):
            remote(src, out.at[peer], w_send.at[k, 0], w_recv.at[k, peer], fsdp=peer).wait_recv()
    not_owner = f != dense_owner
    on(not_owner, dense_sends[0], "wait_recv")
    for copy in own:
        copy.wait()
    on(is_owner, own_dense, "wait")
    for copy in sends + pos_sends:
        copy.wait_send()
    for copy in dense_sends:
        on(is_owner, copy, "wait_send")
    on(has_right, right[0], "wait_send")
    on(has_left, left[0], "wait_send")
    across_left[0].wait_send()
    for k in range(1, chips):
        has_l, has_r = chip >= k, chip + k <= chips - 1

        @pl.when(has_l)
        def _():
            across_left[k].wait_send()

            @pl.when(has_right)
            def _():
                right[k].wait_send()

        @pl.when(has_r)
        def _():
            across_right[k].wait_send()

            @pl.when(has_left)
            def _():
                left[k].wait_send()


def gather_all(hidden, positions, vectors, qkv_own, up_own, down_weight, dense_weight, ff_piece):
    sp, fsdp = lax.axis_size("sp"), lax.axis_size("fsdp")
    bf16 = jnp.bfloat16
    width = down_weight.shape[1]
    shapes = (
        ((sp,) + hidden.shape, bf16),
        ((sp,) + positions.shape, jnp.int32),
        ((fsdp,) + vectors.shape, bf16),
        ((fsdp,) + qkv_own.shape, bf16),
        ((fsdp,) + up_own.shape, bf16),
        ((fsdp, ff_piece, width), bf16),
        ((width // sp, width), bf16),
    )
    dma = pltpu.SemaphoreType.DMA
    return pl.pallas_call(
        functools.partial(gather_kernel, sp, fsdp),
        out_shape=[jax.ShapeDtypeStruct(*shape) for shape in shapes],
        in_specs=[pl.BlockSpec(memory_space=pl.ANY)] * 7,
        out_specs=[pl.BlockSpec(memory_space=pltpu.VMEM)] * 7,
        scratch_shapes=[
            dma((7,)), dma((4, sp // 2)), dma((sp,)), dma((sp,)), dma((sp,)),
            dma((5, fsdp)), dma((5, fsdp)),
        ],
        compiler_params=pltpu.CompilerParams(
            collective_id=1, has_side_effects=True, vmem_limit_bytes=40 << 20
        ),
        name="gather_all",
    )(hidden, positions, vectors, qkv_own, up_own, down_weight, dense_weight)


def reduce_kernel(
    sp, fsdp,
    down_ref, dense_ref, up_ref, qkv_ref, vec_ref,
    down_out, dense_out, up_out, qkv_out, vec_out,
    down_got, dense_got, up_got, qkv_got, vec_got,
    down_sum, up_sum, qkv_sum, vec_sum, vec_two,
    send_one, recv_one, send_two, recv_two, move_send, move_recv, own_sem,
):
    f32, bf16 = jnp.float32, jnp.bfloat16
    s, f = lax.axis_index("sp"), lax.axis_index("fsdp")
    spot = f * sp + s
    rank = s * fsdp + f
    move_sp, move_f = spot // fsdp, spot % fsdp
    moves = spot != rank

    barrier = pltpu.get_barrier_semaphore()
    count = sp + fsdp - 2
    for d in range(1, sp):
        pl.semaphore_signal(barrier, inc=1, device_id={"sp": (s + d) % sp}, device_id_type=MESH)
    for d in range(1, fsdp):
        pl.semaphore_signal(barrier, inc=1, device_id={"fsdp": (f + d) % fsdp}, device_id_type=MESH)

    @pl.when(moves)
    def _():
        pl.semaphore_signal(
            barrier, inc=1,
            device_id={"sp": rank % sp, "fsdp": rank // sp}, device_id_type=MESH,
        )
        pl.semaphore_wait(barrier, count + 1)

    @pl.when(spot == rank)
    def _():
        pl.semaphore_wait(barrier, count)

    stage = [
        (lambda j: up_ref.at[:, j], up_got),
        (lambda j: qkv_ref.at[:, j], qkv_got),
        (lambda j: down_ref.at[j], down_got),
        (lambda j: dense_ref.at[j], dense_got),
        (lambda j: vec_ref.at[:, j], vec_got),
    ]
    sends = []
    for k, (view, got) in enumerate(stage):
        for d in range(1, fsdp):
            peer = (f + d) % fsdp
            sends.append(
                remote(view(peer), got.at[f], send_one.at[k, d], recv_one.at[k, f], fsdp=peer)
            )
            sends[-1].start()

    def collect(k, view):
        got = stage[k][1]
        total = None
        for d in range(1, fsdp):
            peer = (f + d) % fsdp
            remote(
                stage[k][0](peer), got.at[peer], send_one.at[k, 0], recv_one.at[k, peer], fsdp=peer
            ).wait_recv()
        total = view.astype(f32)
        for d in range(1, fsdp):
            total = total + got[(f + d) % fsdp].astype(f32)
        return total

    up_sum[...] = collect(0, up_ref[:, f]).astype(bf16)
    qkv_sum[...] = collect(1, qkv_ref[:, f]).astype(bf16)
    second = []

    def spread(k, source, out):
        for d in range(1, sp):
            peer = (s + d) % sp
            second.append(
                remote(source.at[peer], out.at[s], send_two.at[k, d], recv_two.at[k, s], sp=peer)
            )
            second[-1].start()

    spread(0, up_sum, up_out)
    down_sum[...] = collect(2, down_ref[f]).astype(bf16)
    spread(1, qkv_sum, qkv_out)
    vec_sum[...] = collect(4, vec_ref[:, f])
    move = remote(
        down_sum, down_out, move_send, move_recv, sp=move_sp, fsdp=move_f
    )
    keep = pltpu.make_async_copy(down_sum, down_out, own_sem)
    stays = spot == rank

    @pl.when(moves)
    def _():
        move.start()

    @pl.when(stays)
    def _():
        keep.start()

    dense_out[...] = collect(3, dense_ref[f])
    spread(2, vec_sum, vec_two)
    up_out[s] = up_sum[s]
    qkv_out[s] = qkv_sum[s]
    vec_two[s] = vec_sum[s]

    def arrived(k, source, out):
        for d in range(1, sp):
            peer = (s + d) % sp
            remote(
                source.at[peer], out.at[peer], send_two.at[k, 0], recv_two.at[k, peer], sp=peer
            ).wait_recv()

    arrived(2, vec_sum, vec_two)
    total = vec_two[0]
    for j in range(1, sp):
        total = total + vec_two[j]
    vec_out[...] = total
    arrived(0, up_sum, up_out)
    arrived(1, qkv_sum, qkv_out)

    @pl.when(moves)
    def _():
        move.wait()

    @pl.when(stays)
    def _():
        keep.wait()

    for copy in sends + second:
        copy.wait_send()


def reduce_all(grad_down, grad_dense, grad_up, grad_qkv, vectors):
    sp, fsdp = lax.axis_size("sp"), lax.axis_size("fsdp")
    f32, bf16 = jnp.float32, jnp.bfloat16
    down, dense = grad_down.shape[1:], grad_dense.shape[1:]
    up, qkv, vec = ((sp,) + grad.shape[2:] for grad in (grad_up, grad_qkv, vectors))
    dma = pltpu.SemaphoreType.DMA
    return pl.pallas_call(
        functools.partial(reduce_kernel, sp, fsdp),
        out_shape=[
            jax.ShapeDtypeStruct(down, bf16), jax.ShapeDtypeStruct(dense, f32),
            jax.ShapeDtypeStruct(up, bf16), jax.ShapeDtypeStruct(qkv, bf16),
            jax.ShapeDtypeStruct(vec[1:], f32),
        ],
        in_specs=[pl.BlockSpec(memory_space=pltpu.VMEM)] * 5,
        out_specs=[pl.BlockSpec(memory_space=pltpu.VMEM)] * 5,
        scratch_shapes=[
            pltpu.VMEM((fsdp,) + down, bf16), pltpu.VMEM((fsdp,) + dense, bf16),
            pltpu.VMEM((fsdp,) + up, bf16), pltpu.VMEM((fsdp,) + qkv, bf16),
            pltpu.VMEM((fsdp,) + vec, f32),
            pltpu.VMEM(down, bf16), pltpu.VMEM(up, bf16), pltpu.VMEM(qkv, bf16),
            pltpu.VMEM(vec, f32), pltpu.VMEM(vec, f32),
            dma((5, fsdp)), dma((5, fsdp)), dma((3, sp)), dma((3, sp)), dma, dma, dma,
        ],
        compiler_params=pltpu.CompilerParams(
            collective_id=2, has_side_effects=True, vmem_limit_bytes=40 << 20
        ),
        cost_estimate=pl.CostEstimate(
            flops=0, transcendentals=0, bytes_accessed=150_000_000
        ),
        name="reduce_all",
    )(grad_down, grad_dense, grad_up, grad_qkv, vectors)


def local(
    hidden_in,
    positions,
    out_cotangent,
    attn_gain,
    attn_shift,
    mlp_gain,
    mlp_shift,
    qkv_weight,
    qkv_bias,
    dense_weight,
    dense_bias,
    up_weight,
    up_bias,
    down_weight,
    down_bias,
):
    f32, bf16 = jnp.float32, jnp.bfloat16
    seq_count, local_len, width = hidden_in.shape
    sp_size, fsdp_size = lax.axis_size("sp"), lax.axis_size("fsdp")
    sp_index = lax.axis_index("sp")
    total_len = local_len * sp_size
    rows_all = seq_count * total_len
    own_width = width // fsdp_size
    heads_here = HEADS // sp_size
    qkv_cols = qkv_weight.shape[1] // sp_size
    head_cols = width // sp_size
    ff_all = up_weight.shape[1]
    ff_piece = ff_all // (sp_size * fsdp_size)
    ff_here = ff_piece * fsdp_size
    own_rows = width // (sp_size * fsdp_size)

    vectors = jnp.concatenate(
        [attn_gain, attn_shift, mlp_gain, mlp_shift, dense_bias, down_bias, qkv_bias, up_bias]
    )
    x_all, all_positions, vectors, w_qkv, w_up, w_down, w_dense = gather_all(
        hidden_in,
        positions,
        vectors[None],
        lax.dynamic_slice_in_dim(qkv_weight, sp_index * qkv_cols, qkv_cols, axis=1),
        lax.dynamic_slice_in_dim(
            up_weight.reshape(own_width, fsdp_size, sp_size, ff_piece), sp_index, 1, axis=2
        ).reshape(own_width, ff_here),
        down_weight,
        dense_weight,
        ff_piece,
    )
    cot_own, x_all = lax.optimization_barrier((out_cotangent, x_all))
    cot_all = lax.all_gather(cot_own, "sp", axis=1, tiled=True)
    x_all = x_all.transpose(1, 0, 2, 3).reshape(seq_count, total_len, width)
    all_positions = all_positions.transpose(1, 0, 2).reshape(seq_count, total_len)
    vectors = vectors[:, 0]
    w_qkv = w_qkv.reshape(width, qkv_cols)
    w_up = w_up.reshape(width, ff_here)
    w_down = w_down.reshape(ff_here, width)
    g_attn, s_attn, g_mlp, s_mlp, b_dense, b_down = (
        vectors[:, k * own_width : (k + 1) * own_width].reshape(width) for k in range(6)
    )
    start = 6 * own_width
    own_qkv = qkv_bias.shape[0]
    b_qkv = lax.dynamic_slice_in_dim(
        vectors[:, start : start + own_qkv].reshape(-1), sp_index * qkv_cols, qkv_cols
    )
    b_up = lax.dynamic_slice_in_dim(
        vectors[:, start + own_qkv :], sp_index * ff_piece, ff_piece, axis=1
    ).reshape(ff_here)

    normed_all, _ = layer_norm(x_all.astype(f32).reshape(rows_all, width))
    attn_in = affine(normed_all, g_attn, s_attn).astype(bf16)
    mlp_in = affine(normed_all, g_mlp, s_mlp).astype(bf16)
    cot_rows = cot_all.reshape(rows_all, width)

    joined = jnp.dot(attn_in, w_qkv, preferred_element_type=f32) + b_qkv.astype(f32)
    joined = joined.reshape(seq_count, total_len, heads_here, 3, HD)
    cosine, sine_table = rope_tables(all_positions, ROT)
    head_side = jnp.concatenate(
        [
            rotate(joined[:, :, :, 0], cosine, sine_table, ROT),
            rotate(joined[:, :, :, 1], cosine, sine_table, ROT),
            joined[:, :, :, 2],
        ],
        axis=-1,
    ).astype(bf16)
    mixed_heads, log_total = attend_forward(head_side, all_positions)
    mixed_rows = mixed_heads.reshape(rows_all, head_cols)
    up_out = jnp.dot(mlp_in, w_up, preferred_element_type=f32) + b_up.astype(f32)
    activated, gelu_slope = gelu_pair(up_out)
    activated = activated.astype(bf16)
    out_part = jnp.dot(mixed_rows, w_dense, preferred_element_type=f32) + jnp.dot(
        activated, w_down, preferred_element_type=f32
    )
    out_part, cot_rows = lax.optimization_barrier((out_part.astype(bf16), cot_rows))
    out_sum = lax.psum_scatter(
        out_part.reshape(seq_count, total_len, width),
        "sp", scatter_dimension=1, tiled=True,
    )

    grad_up = jnp.einsum("rd,fd->rf", cot_rows, w_down, preferred_element_type=f32) * gelu_slope
    grad_up_half = grad_up.astype(bf16)
    up_bias_part = jnp.sum(grad_up, axis=0)
    grad_mlp_in = jnp.einsum("rf,df->rd", grad_up_half, w_up, preferred_element_type=f32)
    grad_mixed = jnp.einsum(
        "re,de->rd", cot_rows, w_dense, preferred_element_type=f32
    ).astype(bf16)
    grad_heads = grad_mixed.reshape(seq_count, total_len, heads_here, HD)
    grad_down = jnp.einsum("rf,rd->fd", activated, cot_rows, preferred_element_type=f32)
    grad_dense = jnp.einsum("rd,re->de", mixed_rows, cot_rows, preferred_element_type=f32)
    grad_up_weight = jnp.einsum("rd,rf->df", mlp_in, grad_up_half, preferred_element_type=f32)
    grad_down, grad_dense, grad_up_weight, grad_heads, out_sum = lax.optimization_barrier(
        (
            grad_down.astype(bf16), grad_dense.astype(bf16), grad_up_weight.astype(bf16),
            grad_heads, out_sum,
        )
    )

    x_own = hidden_in.astype(f32)
    block_out = (
        x_own + out_sum.astype(f32) + (b_dense.astype(f32) + b_down.astype(f32))
    ).astype(bf16)
    grad_tokens = attend_backward(head_side, all_positions, grad_heads, log_total).astype(f32)
    grad_joined = jnp.stack(
        [
            rotate_back(grad_tokens[..., :HD], cosine, sine_table, ROT),
            rotate_back(grad_tokens[..., HD : 2 * HD], cosine, sine_table, ROT),
            grad_tokens[..., 2 * HD :],
        ],
        axis=3,
    ).reshape(rows_all, qkv_cols)
    qkv_bias_part = jnp.sum(grad_joined, axis=0)
    grad_joined_half = grad_joined.astype(bf16)
    grad_attn_in = jnp.einsum("rc,dc->rd", grad_joined_half, w_qkv, preferred_element_type=f32)
    normed_part = grad_attn_in * g_attn.astype(f32) + grad_mlp_in * g_mlp.astype(f32)
    normed_part, grad_joined_half = lax.optimization_barrier(
        (normed_part.astype(bf16), grad_joined_half)
    )
    grad_normed = lax.psum_scatter(
        normed_part.reshape(seq_count, total_len, width),
        "sp", scatter_dimension=1, tiled=True,
    ).astype(f32)
    grad_qkv = jnp.einsum(
        "rd,rc->dc", attn_in, grad_joined_half, preferred_element_type=f32
    ).astype(bf16)

    owners = sp_size * fsdp_size
    up_bias_full = lax.dynamic_update_slice_in_dim(
        jnp.zeros((fsdp_size, sp_size, ff_piece), f32),
        up_bias_part.reshape(fsdp_size, 1, ff_piece), sp_index, axis=1,
    ).reshape(owners, ff_piece)
    qkv_bias_full = lax.dynamic_update_slice_in_dim(
        jnp.zeros((sp_size * qkv_cols,), f32), qkv_bias_part, sp_index * qkv_cols, axis=0
    ).reshape(owners, -1)
    grad_own = out_cotangent.astype(f32)
    sums = [
        jnp.sum(grad_attn_in * normed_all, axis=0),
        jnp.sum(grad_attn_in, axis=0),
        jnp.sum(grad_mlp_in * normed_all, axis=0),
        jnp.sum(grad_mlp_in, axis=0),
        jnp.sum(grad_own, axis=(0, 1)),
    ]
    vector_parts = jnp.concatenate(
        [up_bias_full, qkv_bias_full] + [v.reshape(owners, own_rows) for v in sums], axis=1
    )
    down_rows, dense_grad, up_rows, qkv_rows, vector_sums = reduce_all(
        grad_down.reshape(fsdp_size, ff_piece, width),
        grad_dense.reshape(fsdp_size, own_rows, width),
        grad_up_weight.reshape(sp_size, fsdp_size, own_rows, ff_here),
        grad_qkv.reshape(sp_size, fsdp_size, own_rows, qkv_cols),
        vector_parts.reshape(sp_size, fsdp_size, 1, -1),
    )
    down_grad = down_rows.astype(f32)
    up_grad = (
        up_rows.reshape(sp_size, own_rows, fsdp_size, ff_piece)
        .transpose(1, 2, 0, 3)
        .reshape(own_rows, ff_all)
        .astype(f32)
    )
    qkv_grad = (
        qkv_rows.transpose(1, 0, 2).reshape(own_rows, sp_size * qkv_cols).astype(f32)
    )
    vector_sums = vector_sums[0]
    qkv_piece = qkv_cols // fsdp_size
    up_bias_grad = vector_sums[:ff_piece]
    qkv_bias_grad = vector_sums[ff_piece : ff_piece + qkv_piece]
    tail = vector_sums[ff_piece + qkv_piece :]
    attn_gain_grad, attn_shift_grad, mlp_gain_grad, mlp_shift_grad, output_bias_grad = (
        tail[k * own_rows : (k + 1) * own_rows] for k in range(5)
    )

    normed_own, inv_std = layer_norm(x_own)
    mean_grad = jnp.mean(grad_normed, axis=-1, keepdims=True)
    mean_cross = jnp.mean(grad_normed * normed_own, axis=-1, keepdims=True)
    input_grad = grad_own + inv_std * (grad_normed - mean_grad - normed_own * mean_cross)
    return (
        block_out,
        input_grad,
        attn_gain_grad,
        attn_shift_grad,
        mlp_gain_grad,
        mlp_shift_grad,
        qkv_grad,
        qkv_bias_grad,
        dense_grad,
        output_bias_grad,
        up_grad,
        up_bias_grad,
        down_grad,
        output_bias_grad,
    )


def solution(mesh):
    placed = (
        P("fsdp", "sp", None),
        P("fsdp", "sp"),
        P("fsdp", "sp", None),
        P("fsdp"),
        P("fsdp"),
        P("fsdp"),
        P("fsdp"),
        P("fsdp", None),
        P("fsdp"),
        P("fsdp", None),
        P("fsdp"),
        P("fsdp", None),
        P("fsdp"),
        P("fsdp", None),
        P("fsdp"),
    )
    return jax.shard_map(
        local,
        mesh=mesh,
        in_specs=placed,
        out_specs=(
            P("fsdp", "sp", None),
            P("fsdp", "sp", None),
            P(("sp", "fsdp")),
            P(("sp", "fsdp")),
            P(("sp", "fsdp")),
            P(("sp", "fsdp")),
            P(("sp", "fsdp"), None),
            P(("sp", "fsdp")),
            P(("sp", "fsdp"), None),
            P(("sp", "fsdp")),
            P(("sp", "fsdp"), None),
            P(("sp", "fsdp")),
            P(("sp", "fsdp"), None),
            P(("sp", "fsdp")),
        ),
        check_vma=False,
    )
```

```python
import functools
import math

import jax
import jax.numpy as jnp
from jax import lax
from jax.experimental import pallas as pl
from jax.experimental.pallas import tpu as pltpu
from jax.sharding import PartitionSpec as P

HEADS = 16
HD = 64
ROT = 16


NORM_EPS = 1e-05
ROPE_BASE = 10000.0
ROOT_HALF = 0.7071067811865476
INV_ROOT_TWO_PI = 0.3989422804014327
MASK_FILL = -1e30


def layer_norm(values):
    row_mean = jnp.mean(values, axis=-1, keepdims=True)
    centered = values - row_mean
    inv_std = lax.rsqrt(jnp.mean(centered * centered, axis=-1, keepdims=True) + NORM_EPS)
    return (centered * inv_std, inv_std)


def gelu_pair(hidden):
    cdf_part = 0.5 * (1.0 + jax.scipy.special.erf(hidden * ROOT_HALF))
    density = jnp.exp(-0.5 * hidden * hidden) * INV_ROOT_TWO_PI
    return (hidden * cdf_part, cdf_part + hidden * density)


def rope_rows(positions, rot_dims):
    half_dims = rot_dims // 2
    inv_freq = jnp.exp(
        jnp.arange(half_dims, dtype=jnp.float32) * (-2.0 * math.log(ROPE_BASE) / rot_dims)
    )
    angles = inv_freq[:, None] * positions.astype(jnp.float32)[None, :]
    return (jnp.cos(angles), jnp.sin(angles))


def project_kernel(
    heads, x_ref, w_ref, bias_ref, affine_ref, cos_ref, sin_ref,
    attn_out, mlp_out, mean_out, inv_out, q_out, k_out, v_out, qt_out, kt_out, vt_out,
):
    f32, bf16 = jnp.float32, jnp.bfloat16
    values = x_ref[...].astype(f32)
    row_mean = jnp.mean(values, axis=-1, keepdims=True)
    centered = values - row_mean
    inv_std = lax.rsqrt(jnp.mean(centered * centered, axis=-1, keepdims=True) + NORM_EPS)
    normed = centered * inv_std
    mean_out[...] = row_mean
    inv_out[...] = inv_std
    attn_in = (normed * affine_ref[0:1] + affine_ref[1:2]).astype(bf16)
    attn_out[...] = attn_in
    mlp_out[...] = (normed * affine_ref[2:3] + affine_ref[3:4]).astype(bf16)
    joined = jnp.dot(attn_in, w_ref[...], preferred_element_type=f32) + bias_ref[...]
    turned = joined.T
    half = ROT // 2
    cosine, sine = cos_ref[...], sin_ref[...]
    for h in range(heads):
        base = h * 3 * HD
        for j, (out, out_t) in enumerate(((q_out, qt_out), (k_out, kt_out), (v_out, vt_out))):
            rows = turned[base + j * HD : base + (j + 1) * HD]
            if j < 2:
                low, high = rows[:half], rows[half : 2 * half]
                rows = jnp.concatenate(
                    [low * cosine - high * sine, high * cosine + low * sine, rows[2 * half :]],
                    axis=0,
                )
            out_t[h] = rows.astype(bf16)
            out[h] = rows.T.astype(bf16)


def project(x_rows, w_qkv, b_qkv, affine_rows, cosine, sine, heads):
    f32, bf16 = jnp.float32, jnp.bfloat16
    rows_all, width = x_rows.shape
    block = min(256, rows_all)
    cols = w_qkv.shape[1]
    whole = lambda shape: pl.BlockSpec(shape, lambda i: (0,) * len(shape))
    tall = pl.BlockSpec((heads, block, HD), lambda i: (0, i, 0))
    wide = pl.BlockSpec((heads, HD, block), lambda i: (0, 0, i))
    rows = pl.BlockSpec((block, width), lambda i: (i, 0))
    thin = pl.BlockSpec((block, 1), lambda i: (i, 0))
    angle = pl.BlockSpec((ROT // 2, block), lambda i: (0, i))
    shape = jax.ShapeDtypeStruct
    return pl.pallas_call(
        functools.partial(project_kernel, heads),
        grid=(rows_all // block,),
        out_shape=[shape((rows_all, width), bf16)] * 2
        + [shape((rows_all, 1), f32)] * 2
        + [shape((heads, rows_all, HD), bf16)] * 3
        + [shape((heads, HD, rows_all), bf16)] * 3,
        in_specs=[rows, whole((width, cols)), whole((1, cols)), whole((4, width)), angle, angle],
        out_specs=[rows, rows, thin, thin] + [tall] * 3 + [wide] * 3,
        compiler_params=pltpu.CompilerParams(vmem_limit_bytes=40 << 20),
        cost_estimate=pl.CostEstimate(
            flops=2 * rows_all * width * cols, transcendentals=0,
            bytes_accessed=6 * rows_all * width,
        ),
        name="project",
    )(x_rows, w_qkv, b_qkv, affine_rows, cosine, sine)


def allowed_tile(start_row, key_start, query_start, keys, queries):
    key = key_start + lax.broadcasted_iota(jnp.int32, (keys, queries), 0)
    query = query_start + lax.broadcasted_iota(jnp.int32, (1, queries), 1)
    return (key <= query) & (key >= start_row)


def attend_kernel(
    heads, tile_q, tile_k, scale, start_ref, k_ref, qt_ref, vt_ref, mixed_out, exact_out, total_out
):
    f32, bf16 = jnp.float32, jnp.bfloat16
    length = k_ref.shape[1]
    for i in range(length // tile_q):
        span = pl.ds(i * tile_q, tile_q)
        start_row = start_ref[:, span]
        queries = [qt_ref[h, :, span] for h in range(heads)]

        def step(j, carry):
            at = pl.multiple_of(j * tile_k, tile_k)
            allowed = allowed_tile(start_row, at, i * tile_q, tile_k, tile_q)
            result = []
            for h in range(heads):
                top, mass, total = carry[h]
                scores = jnp.dot(
                    k_ref[h, pl.ds(at, tile_k)], queries[h], preferred_element_type=f32
                )
                scores = jnp.where(allowed, scores * scale, MASK_FILL)
                new_top = jnp.maximum(top, jnp.max(scores, axis=0, keepdims=True))
                probs = jnp.exp(scores - new_top)
                shrink = jnp.exp(top - new_top)
                mass = mass * shrink + jnp.sum(probs, axis=0, keepdims=True)
                total = total * shrink + jnp.dot(
                    vt_ref[h, :, pl.ds(at, tile_k)], probs.astype(bf16),
                    preferred_element_type=f32,
                )
                result.append((new_top, mass, total))
            return tuple(result)

        begin = (
            jnp.full((1, tile_q), MASK_FILL, f32),
            jnp.zeros((1, tile_q), f32),
            jnp.zeros((HD, tile_q), f32),
        )
        state = lax.fori_loop(0, (i + 1) * tile_q // tile_k, step, (begin,) * heads)
        for h in range(heads):
            top, mass, total = state[h]
            exact = total / mass
            exact_out[h, :, span] = exact
            mixed_out[h, :, span] = exact.astype(bf16)
            total_out[h, :, span] = top + jnp.log(mass)


def attend_forward(start_row, k, qt, vt):
    f32, bf16 = jnp.float32, jnp.bfloat16
    heads, length, head_dim = k.shape
    shape = jax.ShapeDtypeStruct
    pairs = heads * length * length // 2
    return pl.pallas_call(
        functools.partial(
            attend_kernel, heads, min(512, length), min(256, length), 1.0 / math.sqrt(head_dim)
        ),
        out_shape=[
            shape((heads, head_dim, length), bf16), shape((heads, head_dim, length), f32),
            shape((heads, 1, length), f32),
        ],
        in_specs=[pl.BlockSpec(memory_space=pltpu.VMEM)] * 4,
        out_specs=[pl.BlockSpec(memory_space=pltpu.VMEM)] * 3,
        compiler_params=pltpu.CompilerParams(vmem_limit_bytes=40 << 20),
        cost_estimate=pl.CostEstimate(
            flops=16 * pairs * head_dim, transcendentals=pairs, bytes_accessed=8 * k.size
        ),
        name="attend",
    )(start_row, k, qt, vt)


def attend_back_kernel(
    heads, tile_q, tile_k, scale,
    start_ref, q_ref, k_ref, v_ref, qt_ref, kt_ref, grad_ref, exact_ref, total_ref,
    cos_ref, sin_ref, joined_out, bias_out,
    grad_rows, delta, dq_sum, dk_sum, dv_sum,
):
    f32, bf16 = jnp.float32, jnp.bfloat16
    length = k_ref.shape[1]
    for h in range(heads):
        grad_t = grad_ref[h].astype(f32)
        grad_rows[h] = grad_t.T.astype(bf16)
        delta[h] = jnp.sum(grad_t * exact_ref[h], axis=0, keepdims=True)
    dk_sum[...] = jnp.zeros_like(dk_sum)
    dv_sum[...] = jnp.zeros_like(dv_sum)
    for i in range(length // tile_q):
        span = pl.ds(i * tile_q, tile_q)
        start_row = start_ref[:, span]

        def step(j, carry):
            at = pl.multiple_of(j * tile_k, tile_k)
            keys = pl.ds(at, tile_k)
            allowed = allowed_tile(start_row, at, i * tile_q, tile_k, tile_q)
            result = []
            for h in range(heads):
                scores = jnp.dot(k_ref[h, keys], qt_ref[h, :, span], preferred_element_type=f32)
                grad_probs = jnp.dot(
                    v_ref[h, keys], grad_ref[h, :, span], preferred_element_type=f32
                )
                probs = jnp.exp(
                    jnp.where(allowed, scores * scale, MASK_FILL) - total_ref[h, :, span]
                )
                dv_sum[h, keys] += jnp.dot(
                    probs.astype(bf16), grad_rows[h, span], preferred_element_type=f32
                )
                grad_scores = (scale * probs * (grad_probs - delta[h, :, span])).astype(bf16)
                dk_sum[h, keys] += jnp.dot(
                    grad_scores, q_ref[h, span], preferred_element_type=f32
                )
                result.append(
                    carry[h]
                    + jnp.dot(kt_ref[h, :, keys], grad_scores, preferred_element_type=f32)
                )
            return tuple(result)

        done = lax.fori_loop(
            0, (i + 1) * tile_q // tile_k, step, (jnp.zeros((HD, tile_q), f32),) * heads
        )
        for h in range(heads):
            dq_sum[h, :, span] = done[h]
    half = ROT // 2
    cosine, sine = cos_ref[...], sin_ref[...]
    for h in range(heads):
        base = h * 3 * HD
        parts = (dq_sum[h], dk_sum[h].T, dv_sum[h].T)
        for j, part in enumerate(parts):
            part = part.astype(bf16).astype(f32)
            if j < 2:
                low, high = part[:half], part[half : 2 * half]
                part = jnp.concatenate(
                    [low * cosine + high * sine, high * cosine - low * sine, part[2 * half :]],
                    axis=0,
                )
            rows = pl.ds(base + j * HD, HD)
            joined_out[rows] = part.astype(bf16)
            bias_out[rows] = jnp.sum(part, axis=1, keepdims=True)


def attend_backward(start_row, q, k, v, qt, kt, grad_t, exact, total, cosine, sine):
    f32, bf16 = jnp.float32, jnp.bfloat16
    heads, length, head_dim = k.shape
    shape = jax.ShapeDtypeStruct
    cols = heads * 3 * head_dim
    pairs = heads * length * length // 2
    return pl.pallas_call(
        functools.partial(
            attend_back_kernel, heads, min(512, length), min(256, length),
            1.0 / math.sqrt(head_dim),
        ),
        out_shape=[shape((cols, length), bf16), shape((cols, 1), f32)],
        in_specs=[pl.BlockSpec(memory_space=pltpu.VMEM)] * 11,
        out_specs=[pl.BlockSpec(memory_space=pltpu.VMEM)] * 2,
        scratch_shapes=[
            pltpu.VMEM((heads, length, head_dim), bf16),
            pltpu.VMEM((heads, 1, length), f32),
            pltpu.VMEM((heads, head_dim, length), f32),
            pltpu.VMEM((heads, length, head_dim), f32),
            pltpu.VMEM((heads, length, head_dim), f32),
        ],
        compiler_params=pltpu.CompilerParams(vmem_limit_bytes=48 << 20),
        cost_estimate=pl.CostEstimate(
            flops=40 * pairs * head_dim, transcendentals=pairs, bytes_accessed=24 * k.size
        ),
        name="attend_back",
    )(start_row, q, k, v, qt, kt, grad_t, exact, total, cosine, sine)


MESH = pl.DeviceIdType.MESH


def remote(src, dst, send_sem, recv_sem, **target):
    return pltpu.make_async_remote_copy(
        src_ref=src, dst_ref=dst, send_sem=send_sem, recv_sem=recv_sem,
        device_id=target, device_id_type=MESH,
    )


def entry_barrier(targets):
    barrier = pltpu.get_barrier_semaphore()
    for target in targets:
        pl.semaphore_signal(barrier, inc=1, device_id=target, device_id_type=MESH)
    pl.semaphore_wait(barrier, len(targets))


def gather_kernel(
    sp, fsdp,
    x_ref, pos_ref, vec_ref, qkv_ref, up_ref, down_ref, dense_ref,
    x_out, pos_out, vec_out, qkv_out, up_out, down_out, dense_out,
    own_sem, line_send, x_recv, pos_send, pos_recv, w_send, w_recv,
):
    s, f = lax.axis_index("sp"), lax.axis_index("fsdp")
    chips = sp // 2
    chip, core = s // 2, s % 2
    partner = chip * 2 + (1 - core)
    head_rows = dense_out.shape[0]
    ff_piece = down_out.shape[1]
    dense_owner = s // (sp // fsdp)
    dense_part = s % (sp // fsdp)
    dense_src = dense_ref.at[pl.ds(pl.multiple_of(dense_part * head_rows, head_rows), head_rows)]
    down_src = down_ref.at[pl.ds(pl.multiple_of(s * ff_piece, ff_piece), ff_piece)]
    has_right, has_left = chip < chips - 1, chip > 0

    entry_barrier(
        [{"sp": (s + d) % sp} for d in range(1, sp)]
        + [{"fsdp": (f + d) % fsdp} for d in range(1, fsdp)]
    )

    def x_copy(src, block, sem, target):
        return remote(src, x_out.at[block], sem, x_recv.at[block], sp=target)

    def on(cond, copy, action):
        @pl.when(cond)
        def _():
            getattr(copy, action)()

    right = [x_copy(x_ref, s, line_send.at[0, 0], s + 2)]
    left = [x_copy(x_ref, s, line_send.at[1, 0], s - 2)]
    across_left = [x_copy(x_ref, s, line_send.at[2, 0], partner)]
    across_right = [None]
    on(has_right, right[0], "start")
    on(has_left, left[0], "start")
    across_left[0].start()

    def place(out, slot, cols):
        return out.at[slot] if cols is None else out.at[slot, :, cols]

    qkv_cols = qkv_out.shape[2]
    qkv_src = qkv_ref
    if qkv_ref.shape[1] != qkv_cols:
        qkv_src = qkv_ref.at[:, pl.ds(pl.multiple_of(s * qkv_cols, qkv_cols), qkv_cols)]
    pieces = [(vec_ref, vec_out, None), (qkv_src, qkv_out, None), (down_src, down_out, None)]
    if up_ref.shape[1] != up_out.shape[2]:
        for c in range(fsdp):
            at = pl.multiple_of((c * sp + s) * ff_piece, ff_piece)
            pieces.append(
                (up_ref.at[:, pl.ds(at, ff_piece)], up_out, pl.ds(c * ff_piece, ff_piece))
            )
    else:
        pieces.append((up_ref, up_out, None))
    dense_slot = len(pieces)
    sends = []
    for d in range(1, fsdp):
        peer = (f + d) % fsdp
        for k, (src, out, cols) in enumerate(pieces[:2]):
            sends.append(
                remote(src, place(out, f, cols), w_send.at[k, d], w_recv.at[k, f], fsdp=peer)
            )
    dense_sends = [
        remote(dense_src, dense_out, w_send.at[dense_slot, d], w_recv.at[dense_slot, 0],
               fsdp=(f + d) % fsdp)
        for d in range(1, fsdp)
    ]
    for d in range(1, fsdp):
        peer = (f + d) % fsdp
        for k, (src, out, cols) in enumerate(pieces[2:], 2):
            sends.append(
                remote(src, place(out, f, cols), w_send.at[k, d], w_recv.at[k, f], fsdp=peer)
            )
    for copy in sends[: 2 * (fsdp - 1)]:
        copy.start()
    is_owner = f == dense_owner
    for copy in dense_sends:
        on(is_owner, copy, "start")
    for copy in sends[2 * (fsdp - 1) :]:
        copy.start()
    pos_sends = []
    for d in range(1, sp):
        peer = (s + d) % sp
        pos_sends.append(remote(pos_ref, pos_out.at[s], pos_send.at[d], pos_recv.at[s], sp=peer))
        pos_sends[-1].start()
    own = [
        pltpu.make_async_copy(src, place(out, f, cols), own_sem.at[k])
        for k, (src, out, cols) in enumerate(pieces)
    ]
    own_dense = pltpu.make_async_copy(dense_src, dense_out, own_sem.at[dense_slot])
    own.append(pltpu.make_async_copy(x_ref, x_out.at[s], own_sem.at[dense_slot + 1]))
    own.append(pltpu.make_async_copy(pos_ref, pos_out.at[s], own_sem.at[dense_slot + 2]))
    for copy in own:
        copy.start()
    on(is_owner, own_dense, "start")

    for k in range(1, chips):
        from_left, from_right = s - 2 * k, s + 2 * k
        has_l, has_r = chip >= k, chip + k <= chips - 1
        held_l, held_r = x_out.at[from_left], x_out.at[from_right]
        right.append(x_copy(held_l, from_left, line_send.at[0, k], s + 2))
        left.append(x_copy(held_r, from_right, line_send.at[1, k], s - 2))
        across_left.append(x_copy(held_l, from_left, line_send.at[2, k], partner))
        across_right.append(x_copy(held_r, from_right, line_send.at[3, k], partner))

        @pl.when(has_l)
        def _():
            across_left[k].wait_recv()

            @pl.when(has_right)
            def _():
                right[k].start()

            across_left[k].start()

        @pl.when(has_r)
        def _():
            across_right[k].wait_recv()

            @pl.when(has_left)
            def _():
                left[k].start()

            across_right[k].start()

    for c in range(chips):
        block = 2 * c + (1 - core)
        x_copy(x_ref, block, line_send.at[0, 0], partner).wait_recv()
    for d in range(1, sp):
        block = (s + d) % sp
        remote(pos_ref, pos_out.at[block], pos_send.at[0], pos_recv.at[block], sp=block).wait_recv()
    for d in range(1, fsdp):
        peer = (f + d) % fsdp
        for k, (src, out, cols) in enumerate(pieces):
            remote(
                src, place(out, peer, cols), w_send.at[k, 0], w_recv.at[k, peer], fsdp=peer
            ).wait_recv()
    not_owner = f != dense_owner
    on(not_owner, dense_sends[0], "wait_recv")
    for copy in own:
        copy.wait()
    on(is_owner, own_dense, "wait")
    for copy in sends + pos_sends:
        copy.wait_send()
    for copy in dense_sends:
        on(is_owner, copy, "wait_send")
    on(has_right, right[0], "wait_send")
    on(has_left, left[0], "wait_send")
    across_left[0].wait_send()
    for k in range(1, chips):
        has_l, has_r = chip >= k, chip + k <= chips - 1

        @pl.when(has_l)
        def _():
            across_left[k].wait_send()

            @pl.when(has_right)
            def _():
                right[k].wait_send()

        @pl.when(has_r)
        def _():
            across_right[k].wait_send()

            @pl.when(has_left)
            def _():
                left[k].wait_send()


def gather_all(
    hidden, positions, vectors, qkv_own, up_own, down_weight, dense_weight, qkv_cols, ff_piece
):
    sp, fsdp = lax.axis_size("sp"), lax.axis_size("fsdp")
    bf16 = jnp.bfloat16
    width = down_weight.shape[1]
    shapes = (
        ((sp,) + hidden.shape, bf16),
        ((sp,) + positions.shape, jnp.int32),
        ((fsdp,) + vectors.shape, bf16),
        ((fsdp, qkv_own.shape[0], qkv_cols), bf16),
        ((fsdp, up_own.shape[0], ff_piece * fsdp), bf16),
        ((fsdp, ff_piece, width), bf16),
        ((width // sp, width), bf16),
    )
    dma = pltpu.SemaphoreType.DMA
    return pl.pallas_call(
        functools.partial(gather_kernel, sp, fsdp),
        out_shape=[jax.ShapeDtypeStruct(*shape) for shape in shapes],
        in_specs=[pl.BlockSpec(memory_space=pl.ANY)] * 7,
        out_specs=[pl.BlockSpec(memory_space=pltpu.VMEM)] * 7,
        scratch_shapes=[
            dma((fsdp + 6,)), dma((4, sp // 2)), dma((sp,)), dma((sp,)), dma((sp,)),
            dma((fsdp + 4, fsdp)), dma((fsdp + 4, fsdp)),
        ],
        compiler_params=pltpu.CompilerParams(
            collective_id=1, has_side_effects=True, vmem_limit_bytes=40 << 20
        ),
        name="gather_all",
    )(hidden, positions, vectors, qkv_own, up_own, down_weight, dense_weight)


def reduce_kernel(
    sp, fsdp,
    down_ref, dense_ref, up_ref, qkv_ref, vec_ref,
    down_out, dense_out, up_out, qkv_out, vec_out,
    down_got, dense_got, up_got, qkv_got, vec_got,
    down_sum, up_sum, qkv_sum, vec_sum, vec_two,
    send_one, recv_one, send_two, recv_two, move_send, move_recv, own_sem,
):
    f32, bf16 = jnp.float32, jnp.bfloat16
    s, f = lax.axis_index("sp"), lax.axis_index("fsdp")
    spot = f * sp + s
    rank = s * fsdp + f
    move_sp, move_f = spot // fsdp, spot % fsdp
    moves = spot != rank

    barrier = pltpu.get_barrier_semaphore()
    count = sp + fsdp - 2
    for d in range(1, sp):
        pl.semaphore_signal(barrier, inc=1, device_id={"sp": (s + d) % sp}, device_id_type=MESH)
    for d in range(1, fsdp):
        pl.semaphore_signal(barrier, inc=1, device_id={"fsdp": (f + d) % fsdp}, device_id_type=MESH)

    @pl.when(moves)
    def _():
        pl.semaphore_signal(
            barrier, inc=1,
            device_id={"sp": rank % sp, "fsdp": rank // sp}, device_id_type=MESH,
        )
        pl.semaphore_wait(barrier, count + 1)

    @pl.when(spot == rank)
    def _():
        pl.semaphore_wait(barrier, count)

    stage = [
        (lambda j: up_ref.at[:, j], up_got),
        (lambda j: qkv_ref.at[:, j], qkv_got),
        (lambda j: down_ref.at[j], down_got),
        (lambda j: dense_ref.at[j], dense_got),
        (lambda j: vec_ref.at[:, j], vec_got),
    ]
    sends = []
    for k, (view, got) in enumerate(stage):
        for d in range(1, fsdp):
            peer = (f + d) % fsdp
            sends.append(
                remote(view(peer), got.at[f], send_one.at[k, d], recv_one.at[k, f], fsdp=peer)
            )
            sends[-1].start()

    def collect(k, view):
        got = stage[k][1]
        total = None
        for d in range(1, fsdp):
            peer = (f + d) % fsdp
            remote(
                stage[k][0](peer), got.at[peer], send_one.at[k, 0], recv_one.at[k, peer], fsdp=peer
            ).wait_recv()
        total = view.astype(f32)
        for d in range(1, fsdp):
            total = total + got[(f + d) % fsdp].astype(f32)
        return total

    up_sum[...] = collect(0, up_ref[:, f]).astype(bf16)
    qkv_sum[...] = collect(1, qkv_ref[:, f]).astype(bf16)
    second = []

    def spread(k, source, out):
        for d in range(1, sp):
            peer = (s + d) % sp
            second.append(
                remote(source.at[peer], out.at[s], send_two.at[k, d], recv_two.at[k, s], sp=peer)
            )
            second[-1].start()

    spread(0, up_sum, up_out)
    down_sum[...] = collect(2, down_ref[f]).astype(bf16)
    spread(1, qkv_sum, qkv_out)
    vec_sum[...] = collect(4, vec_ref[:, f])
    move = remote(
        down_sum, down_out, move_send, move_recv, sp=move_sp, fsdp=move_f
    )
    keep = pltpu.make_async_copy(down_sum, down_out, own_sem)
    stays = spot == rank

    @pl.when(moves)
    def _():
        move.start()

    @pl.when(stays)
    def _():
        keep.start()

    dense_out[...] = collect(3, dense_ref[f])
    spread(2, vec_sum, vec_two)
    up_out[s] = up_sum[s]
    qkv_out[s] = qkv_sum[s]
    vec_two[s] = vec_sum[s]

    def arrived(k, source, out):
        for d in range(1, sp):
            peer = (s + d) % sp
            remote(
                source.at[peer], out.at[peer], send_two.at[k, 0], recv_two.at[k, peer], sp=peer
            ).wait_recv()

    arrived(2, vec_sum, vec_two)
    total = vec_two[0]
    for j in range(1, sp):
        total = total + vec_two[j]
    vec_out[...] = total
    arrived(0, up_sum, up_out)
    arrived(1, qkv_sum, qkv_out)

    @pl.when(moves)
    def _():
        move.wait()

    @pl.when(stays)
    def _():
        keep.wait()

    for copy in sends + second:
        copy.wait_send()


def reduce_all(grad_down, grad_dense, grad_up, grad_qkv, vectors):
    sp, fsdp = lax.axis_size("sp"), lax.axis_size("fsdp")
    f32, bf16 = jnp.float32, jnp.bfloat16
    down, dense = grad_down.shape[1:], grad_dense.shape[1:]
    up, qkv, vec = ((sp,) + grad.shape[2:] for grad in (grad_up, grad_qkv, vectors))
    dma = pltpu.SemaphoreType.DMA
    return pl.pallas_call(
        functools.partial(reduce_kernel, sp, fsdp),
        out_shape=[
            jax.ShapeDtypeStruct(down, bf16), jax.ShapeDtypeStruct(dense, f32),
            jax.ShapeDtypeStruct(up, bf16), jax.ShapeDtypeStruct(qkv, bf16),
            jax.ShapeDtypeStruct(vec[1:], f32),
        ],
        in_specs=[pl.BlockSpec(memory_space=pltpu.VMEM)] * 5,
        out_specs=[pl.BlockSpec(memory_space=pltpu.VMEM)] * 5,
        scratch_shapes=[
            pltpu.VMEM((fsdp,) + down, bf16), pltpu.VMEM((fsdp,) + dense, bf16),
            pltpu.VMEM((fsdp,) + up, bf16), pltpu.VMEM((fsdp,) + qkv, bf16),
            pltpu.VMEM((fsdp,) + vec, f32),
            pltpu.VMEM(down, bf16), pltpu.VMEM(up, bf16), pltpu.VMEM(qkv, bf16),
            pltpu.VMEM(vec, f32), pltpu.VMEM(vec, f32),
            dma((5, fsdp)), dma((5, fsdp)), dma((3, sp)), dma((3, sp)), dma, dma, dma,
        ],
        compiler_params=pltpu.CompilerParams(
            collective_id=2, has_side_effects=True, vmem_limit_bytes=40 << 20
        ),
        cost_estimate=pl.CostEstimate(
            flops=0, transcendentals=0, bytes_accessed=150_000_000
        ),
        name="reduce_all",
    )(grad_down, grad_dense, grad_up, grad_qkv, vectors)


def local(
    hidden_in,
    positions,
    out_cotangent,
    attn_gain,
    attn_shift,
    mlp_gain,
    mlp_shift,
    qkv_weight,
    qkv_bias,
    dense_weight,
    dense_bias,
    up_weight,
    up_bias,
    down_weight,
    down_bias,
):
    f32, bf16 = jnp.float32, jnp.bfloat16
    seq_count, local_len, width = hidden_in.shape
    sp_size, fsdp_size = lax.axis_size("sp"), lax.axis_size("fsdp")
    sp_index = lax.axis_index("sp")
    total_len = local_len * sp_size
    rows_all = seq_count * total_len
    own_width = width // fsdp_size
    heads_here = HEADS // sp_size
    qkv_cols = qkv_weight.shape[1] // sp_size
    head_cols = width // sp_size
    ff_all = up_weight.shape[1]
    ff_piece = ff_all // (sp_size * fsdp_size)
    ff_here = ff_piece * fsdp_size
    own_rows = width // (sp_size * fsdp_size)

    qkv_own, up_own = qkv_weight, up_weight
    if qkv_cols % 128:
        qkv_own = lax.dynamic_slice_in_dim(qkv_weight, sp_index * qkv_cols, qkv_cols, axis=1)
    if ff_piece % 128:
        up_own = lax.dynamic_slice_in_dim(
            up_weight.reshape(own_width, fsdp_size, sp_size, ff_piece), sp_index, 1, axis=2
        ).reshape(own_width, ff_here)
    vectors = jnp.concatenate(
        [attn_gain, attn_shift, mlp_gain, mlp_shift, dense_bias, down_bias, qkv_bias, up_bias]
    )
    x_all, all_positions, vectors, w_qkv, w_up, w_down, w_dense = gather_all(
        hidden_in,
        positions,
        vectors[None],
        qkv_own,
        up_own,
        down_weight,
        dense_weight,
        qkv_cols,
        ff_piece,
    )
    cot_own, x_all = lax.optimization_barrier((out_cotangent, x_all))
    cot_all = lax.all_gather(cot_own, "sp", axis=1, tiled=True)
    x_all = x_all.transpose(1, 0, 2, 3).reshape(seq_count, total_len, width)
    all_positions = all_positions.transpose(1, 0, 2).reshape(seq_count, total_len)
    vectors = vectors[:, 0]
    w_qkv = w_qkv.reshape(width, qkv_cols)
    w_up = w_up.reshape(width, ff_here)
    w_down = w_down.reshape(ff_here, width)
    g_attn, s_attn, g_mlp, s_mlp, b_dense, b_down = (
        vectors[:, k * own_width : (k + 1) * own_width].reshape(width) for k in range(6)
    )
    start = 6 * own_width
    own_qkv = qkv_bias.shape[0]
    b_qkv = lax.dynamic_slice_in_dim(
        vectors[:, start : start + own_qkv].reshape(-1), sp_index * qkv_cols, qkv_cols
    )
    b_up = lax.dynamic_slice_in_dim(
        vectors[:, start + own_qkv :], sp_index * ff_piece, ff_piece, axis=1
    ).reshape(ff_here)

    cot_rows = cot_all.reshape(rows_all, width)
    flat_positions = all_positions.reshape(rows_all)
    cosine, sine = rope_rows(flat_positions, ROT)
    start_row = (jnp.arange(rows_all, dtype=jnp.int32) - flat_positions)[None]
    affine_rows = jnp.stack([g_attn, s_attn, g_mlp, s_mlp]).astype(f32)
    x_rows = x_all.reshape(rows_all, width)
    attn_in, mlp_in, row_mean, row_inv, q, k, v, qt, kt, vt = project(
        x_rows, w_qkv, b_qkv.astype(f32)[None], affine_rows, cosine, sine, heads_here
    )
    mixed_t, exact, log_total = attend_forward(start_row, k, qt, vt)
    mixed_t = mixed_t.reshape(head_cols, rows_all)
    up_out = jnp.dot(mlp_in, w_up, preferred_element_type=f32) + b_up.astype(f32)
    activated, gelu_slope = gelu_pair(up_out)
    activated = activated.astype(bf16)
    out_part = jnp.einsum("dr,de->re", mixed_t, w_dense, preferred_element_type=f32) + jnp.dot(
        activated, w_down, preferred_element_type=f32
    )
    out_part, cot_rows = lax.optimization_barrier((out_part.astype(bf16), cot_rows))
    out_sum = lax.psum_scatter(
        out_part.reshape(seq_count, total_len, width),
        "sp", scatter_dimension=1, tiled=True,
    )

    grad_up = jnp.einsum("rd,fd->rf", cot_rows, w_down, preferred_element_type=f32) * gelu_slope
    grad_up_half = grad_up.astype(bf16)
    up_bias_part = jnp.sum(grad_up, axis=0)
    grad_mlp_in = jnp.einsum("rf,df->rd", grad_up_half, w_up, preferred_element_type=f32)
    grad_heads = (
        jnp.einsum("de,re->dr", w_dense, cot_rows, preferred_element_type=f32)
        .astype(bf16)
        .reshape(heads_here, HD, rows_all)
    )
    grad_down = jnp.einsum("rf,rd->fd", activated, cot_rows, preferred_element_type=f32)
    grad_dense = jnp.einsum("dr,re->de", mixed_t, cot_rows, preferred_element_type=f32)
    grad_up_weight = jnp.einsum("rd,rf->df", mlp_in, grad_up_half, preferred_element_type=f32)
    own_sum = jnp.sum(out_cotangent.astype(f32), axis=(0, 1))
    grad_down, grad_dense, grad_up_weight, grad_heads, own_sum = lax.optimization_barrier(
        (
            grad_down.astype(bf16), grad_dense.astype(bf16), grad_up_weight.astype(bf16),
            grad_heads, own_sum,
        )
    )
    joined_half, qkv_bias_part = attend_backward(
        start_row, q, k, v, qt, kt, grad_heads, exact, log_total, cosine, sine
    )
    joined_half, out_sum = lax.optimization_barrier((joined_half, out_sum))
    qkv_bias_part = qkv_bias_part.reshape(qkv_cols)

    x_own = hidden_in.astype(f32)
    block_out = (
        x_own + out_sum.astype(f32) + (b_dense.astype(f32) + b_down.astype(f32))
    ).astype(bf16)
    grad_attn_in = jnp.einsum("cr,dc->rd", joined_half, w_qkv, preferred_element_type=f32)
    normed_part = grad_attn_in * g_attn.astype(f32) + grad_mlp_in * g_mlp.astype(f32)
    normed_part, joined_half = lax.optimization_barrier(
        (normed_part.astype(bf16), joined_half)
    )
    grad_normed = lax.psum_scatter(
        normed_part.reshape(seq_count, total_len, width),
        "sp", scatter_dimension=1, tiled=True,
    ).astype(f32)
    grad_qkv = jnp.einsum(
        "rd,cr->dc", attn_in, joined_half, preferred_element_type=f32
    ).astype(bf16)

    owners = sp_size * fsdp_size
    up_bias_full = lax.dynamic_update_slice_in_dim(
        jnp.zeros((fsdp_size, sp_size, ff_piece), f32),
        up_bias_part.reshape(fsdp_size, 1, ff_piece), sp_index, axis=1,
    ).reshape(owners, ff_piece)
    qkv_bias_full = lax.dynamic_update_slice_in_dim(
        jnp.zeros((sp_size * qkv_cols,), f32), qkv_bias_part, sp_index * qkv_cols, axis=0
    ).reshape(owners, -1)
    grad_own = out_cotangent.astype(f32)
    normed_all = (x_rows.astype(f32) - row_mean) * row_inv
    sums = [
        jnp.sum(grad_attn_in * normed_all, axis=0),
        jnp.sum(grad_attn_in, axis=0),
        jnp.sum(grad_mlp_in * normed_all, axis=0),
        jnp.sum(grad_mlp_in, axis=0),
        own_sum,
    ]
    vector_parts = jnp.concatenate(
        [up_bias_full, qkv_bias_full] + [v.reshape(owners, own_rows) for v in sums], axis=1
    )
    down_rows, dense_grad, up_rows, qkv_rows, vector_sums = reduce_all(
        grad_down.reshape(fsdp_size, ff_piece, width),
        grad_dense.reshape(fsdp_size, own_rows, width),
        grad_up_weight.reshape(sp_size, fsdp_size, own_rows, ff_here),
        grad_qkv.reshape(sp_size, fsdp_size, own_rows, qkv_cols),
        vector_parts.reshape(sp_size, fsdp_size, 1, -1),
    )
    down_grad = down_rows.astype(f32)
    up_grad = (
        up_rows.reshape(sp_size, own_rows, fsdp_size, ff_piece)
        .transpose(1, 2, 0, 3)
        .reshape(own_rows, ff_all)
        .astype(f32)
    )
    qkv_grad = (
        qkv_rows.transpose(1, 0, 2).reshape(own_rows, sp_size * qkv_cols).astype(f32)
    )
    vector_sums = vector_sums[0]
    qkv_piece = qkv_cols // fsdp_size
    up_bias_grad = vector_sums[:ff_piece]
    qkv_bias_grad = vector_sums[ff_piece : ff_piece + qkv_piece]
    tail = vector_sums[ff_piece + qkv_piece :]
    attn_gain_grad, attn_shift_grad, mlp_gain_grad, mlp_shift_grad, output_bias_grad = (
        tail[k * own_rows : (k + 1) * own_rows] for k in range(5)
    )

    normed_own, inv_std = layer_norm(x_own)
    mean_grad = jnp.mean(grad_normed, axis=-1, keepdims=True)
    mean_cross = jnp.mean(grad_normed * normed_own, axis=-1, keepdims=True)
    input_grad = grad_own + inv_std * (grad_normed - mean_grad - normed_own * mean_cross)
    return (
        block_out,
        input_grad,
        attn_gain_grad,
        attn_shift_grad,
        mlp_gain_grad,
        mlp_shift_grad,
        qkv_grad,
        qkv_bias_grad,
        dense_grad,
        output_bias_grad,
        up_grad,
        up_bias_grad,
        down_grad,
        output_bias_grad,
    )


def solution(mesh):
    placed = (
        P("fsdp", "sp", None),
        P("fsdp", "sp"),
        P("fsdp", "sp", None),
        P("fsdp"),
        P("fsdp"),
        P("fsdp"),
        P("fsdp"),
        P("fsdp", None),
        P("fsdp"),
        P("fsdp", None),
        P("fsdp"),
        P("fsdp", None),
        P("fsdp"),
        P("fsdp", None),
        P("fsdp"),
    )
    return jax.shard_map(
        local,
        mesh=mesh,
        in_specs=placed,
        out_specs=(
            P("fsdp", "sp", None),
            P("fsdp", "sp", None),
            P(("sp", "fsdp")),
            P(("sp", "fsdp")),
            P(("sp", "fsdp")),
            P(("sp", "fsdp")),
            P(("sp", "fsdp"), None),
            P(("sp", "fsdp")),
            P(("sp", "fsdp"), None),
            P(("sp", "fsdp")),
            P(("sp", "fsdp"), None),
            P(("sp", "fsdp")),
            P(("sp", "fsdp"), None),
            P(("sp", "fsdp")),
        ),
        check_vma=False,
    )
```

```python
import functools
import math

import jax
import jax.numpy as jnp
from jax import lax
from jax.experimental import pallas as pl
from jax.experimental.pallas import tpu as pltpu
from jax.sharding import PartitionSpec as P

HEADS = 16
HD = 64
ROT = 16


NORM_EPS = 1e-05
ROPE_BASE = 10000.0
ROOT_HALF = 0.7071067811865476
INV_ROOT_TWO_PI = 0.3989422804014327
MASK_FILL = -1e30


def layer_norm(values):
    row_mean = jnp.mean(values, axis=-1, keepdims=True)
    centered = values - row_mean
    inv_std = lax.rsqrt(jnp.mean(centered * centered, axis=-1, keepdims=True) + NORM_EPS)
    return (centered * inv_std, inv_std)


def gelu_pair(hidden):
    cdf_part = 0.5 * (1.0 + jax.scipy.special.erf(hidden * ROOT_HALF))
    density = jnp.exp(-0.5 * hidden * hidden) * INV_ROOT_TWO_PI
    return (hidden * cdf_part, cdf_part + hidden * density)


def rope_rows(positions, rot_dims):
    half_dims = rot_dims // 2
    inv_freq = jnp.exp(
        jnp.arange(half_dims, dtype=jnp.float32) * (-2.0 * math.log(ROPE_BASE) / rot_dims)
    )
    angles = inv_freq[:, None] * positions.astype(jnp.float32)[None, :]
    return (jnp.cos(angles), jnp.sin(angles))


def project_kernel(
    heads, x_ref, w_ref, bias_ref, affine_ref, cos_ref, sin_ref,
    attn_out, mlp_out, mean_out, inv_out, q_out, k_out, v_out, qt_out, kt_out, vt_out,
):
    f32, bf16 = jnp.float32, jnp.bfloat16
    values = x_ref[...].astype(f32)
    row_mean = jnp.mean(values, axis=-1, keepdims=True)
    centered = values - row_mean
    inv_std = lax.rsqrt(jnp.mean(centered * centered, axis=-1, keepdims=True) + NORM_EPS)
    normed = centered * inv_std
    mean_out[...] = row_mean
    inv_out[...] = inv_std
    attn_in = (normed * affine_ref[0:1] + affine_ref[1:2]).astype(bf16)
    attn_out[...] = attn_in
    mlp_out[...] = (normed * affine_ref[2:3] + affine_ref[3:4]).astype(bf16)
    joined = jnp.dot(attn_in, w_ref[...], preferred_element_type=f32) + bias_ref[...]
    turned = joined.T
    half = ROT // 2
    cosine, sine = cos_ref[...], sin_ref[...]
    for h in range(heads):
        base = h * 3 * HD
        for j, (out, out_t) in enumerate(((q_out, qt_out), (k_out, kt_out), (v_out, vt_out))):
            rows = turned[base + j * HD : base + (j + 1) * HD]
            if j < 2:
                low, high = rows[:half], rows[half : 2 * half]
                rows = jnp.concatenate(
                    [low * cosine - high * sine, high * cosine + low * sine, rows[2 * half :]],
                    axis=0,
                )
            out_t[h] = rows.astype(bf16)
            out[h] = rows.T.astype(bf16)


def project(x_rows, w_qkv, b_qkv, affine_rows, cosine, sine, heads):
    f32, bf16 = jnp.float32, jnp.bfloat16
    rows_all, width = x_rows.shape
    block = min(256, rows_all)
    cols = w_qkv.shape[1]
    whole = lambda shape: pl.BlockSpec(shape, lambda i: (0,) * len(shape))
    tall = pl.BlockSpec((heads, block, HD), lambda i: (0, i, 0))
    wide = pl.BlockSpec((heads, HD, block), lambda i: (0, 0, i))
    rows = pl.BlockSpec((block, width), lambda i: (i, 0))
    thin = pl.BlockSpec((block, 1), lambda i: (i, 0))
    angle = pl.BlockSpec((ROT // 2, block), lambda i: (0, i))
    shape = jax.ShapeDtypeStruct
    return pl.pallas_call(
        functools.partial(project_kernel, heads),
        grid=(rows_all // block,),
        out_shape=[shape((rows_all, width), bf16)] * 2
        + [shape((rows_all, 1), f32)] * 2
        + [shape((heads, rows_all, HD), bf16)] * 3
        + [shape((heads, HD, rows_all), bf16)] * 3,
        in_specs=[rows, whole((width, cols)), whole((1, cols)), whole((4, width)), angle, angle],
        out_specs=[rows, rows, thin, thin] + [tall] * 3 + [wide] * 3,
        compiler_params=pltpu.CompilerParams(vmem_limit_bytes=40 << 20),
        cost_estimate=pl.CostEstimate(
            flops=2 * rows_all * width * cols, transcendentals=0,
            bytes_accessed=6 * rows_all * width,
        ),
        name="project",
    )(x_rows, w_qkv, b_qkv, affine_rows, cosine, sine)


def allowed_tile(start_row, key_start, query_start, keys, queries):
    key = key_start + lax.broadcasted_iota(jnp.int32, (keys, queries), 0)
    query = query_start + lax.broadcasted_iota(jnp.int32, (1, queries), 1)
    return (key <= query) & (key >= start_row)


def attend_kernel(
    heads, tile_q, tile_k, scale, start_ref, k_ref, qt_ref, vt_ref, mixed_out, exact_out, total_out
):
    f32, bf16 = jnp.float32, jnp.bfloat16
    length = k_ref.shape[1]
    for i in range(length // tile_q):
        span = pl.ds(i * tile_q, tile_q)
        start_row = start_ref[:, span]
        queries = [qt_ref[h, :, span] for h in range(heads)]

        def step(j, carry):
            at = pl.multiple_of(j * tile_k, tile_k)
            allowed = allowed_tile(start_row, at, i * tile_q, tile_k, tile_q)
            result = []
            for h in range(heads):
                top, mass, total = carry[h]
                scores = jnp.dot(
                    k_ref[h, pl.ds(at, tile_k)], queries[h], preferred_element_type=f32
                )
                scores = jnp.where(allowed, scores * scale, MASK_FILL)
                new_top = jnp.maximum(top, jnp.max(scores, axis=0, keepdims=True))
                probs = jnp.exp(scores - new_top)
                shrink = jnp.exp(top - new_top)
                mass = mass * shrink + jnp.sum(probs, axis=0, keepdims=True)
                total = total * shrink + jnp.dot(
                    vt_ref[h, :, pl.ds(at, tile_k)], probs.astype(bf16),
                    preferred_element_type=f32,
                )
                result.append((new_top, mass, total))
            return tuple(result)

        begin = (
            jnp.full((1, tile_q), MASK_FILL, f32),
            jnp.zeros((1, tile_q), f32),
            jnp.zeros((HD, tile_q), f32),
        )
        state = lax.fori_loop(0, (i + 1) * tile_q // tile_k, step, (begin,) * heads)
        for h in range(heads):
            top, mass, total = state[h]
            exact = total / mass
            exact_out[h, :, span] = exact
            mixed_out[h, :, span] = exact.astype(bf16)
            total_out[h, :, span] = top + jnp.log(mass)


def attend_forward(start_row, k, qt, vt):
    f32, bf16 = jnp.float32, jnp.bfloat16
    heads, length, head_dim = k.shape
    shape = jax.ShapeDtypeStruct
    pairs = heads * length * length // 2
    return pl.pallas_call(
        functools.partial(
            attend_kernel, heads, min(512, length), min(256, length), 1.0 / math.sqrt(head_dim)
        ),
        out_shape=[
            shape((heads, head_dim, length), bf16), shape((heads, head_dim, length), f32),
            shape((heads, 1, length), f32),
        ],
        in_specs=[pl.BlockSpec(memory_space=pltpu.VMEM)] * 4,
        out_specs=[pl.BlockSpec(memory_space=pltpu.VMEM)] * 3,
        compiler_params=pltpu.CompilerParams(vmem_limit_bytes=40 << 20),
        cost_estimate=pl.CostEstimate(
            flops=16 * pairs * head_dim, transcendentals=pairs, bytes_accessed=8 * k.size
        ),
        name="attend",
    )(start_row, k, qt, vt)


def attend_back_kernel(
    heads, tile_q, tile_k, scale, sp, fsdp,
    up_ref, down_ref, dense_ref, start_ref, q_ref, k_ref, v_ref, qt_ref, kt_ref, grad_ref, exact_ref, total_ref,
    cos_ref, sin_ref, joined_out, bias_out, up_out, down_out, dense_out,
    grad_rows, delta, dq_sum, dk_sum, dv_sum,
    up_got, down_got, dense_got, up_sum, down_sum,
    send_one, recv_one, send_two, recv_two, move_send, move_recv, own_sem,
):
    f32, bf16 = jnp.float32, jnp.bfloat16
    length = k_ref.shape[1]
    s, f = lax.axis_index("sp"), lax.axis_index("fsdp")
    spot, rank = f * sp + s, s * fsdp + f
    barrier = pltpu.get_barrier_semaphore()
    count = sp + fsdp - 2
    for d in range(1, sp):
        pl.semaphore_signal(barrier, inc=1, device_id={"sp": (s + d) % sp}, device_id_type=MESH)
    for d in range(1, fsdp):
        pl.semaphore_signal(barrier, inc=1, device_id={"fsdp": (f + d) % fsdp}, device_id_type=MESH)

    @pl.when(spot != rank)
    def _():
        pl.semaphore_signal(
            barrier, inc=1,
            device_id={"sp": rank % sp, "fsdp": rank // sp}, device_id_type=MESH,
        )
        pl.semaphore_wait(barrier, count + 1)

    @pl.when(spot == rank)
    def _():
        pl.semaphore_wait(barrier, count)

    views = [lambda j: up_ref.at[:, j], lambda j: down_ref.at[j], lambda j: dense_ref.at[j]]
    gots = [up_got, down_got, dense_got]
    one, two = (send_one, recv_one), (send_two, recv_two)
    sends = start_stage(views, gots, f, fsdp, *one)
    for h in range(heads):
        grad_t = grad_ref[h].astype(f32)
        grad_rows[h] = grad_t.T.astype(bf16)
        delta[h] = jnp.sum(grad_t * exact_ref[h], axis=0, keepdims=True)
    dk_sum[...] = jnp.zeros_like(dk_sum)
    dv_sum[...] = jnp.zeros_like(dv_sum)
    blocks = length // tile_q
    for i in reversed(range(blocks)):
        span = pl.ds(i * tile_q, tile_q)
        start_row = start_ref[:, span]

        def step(j, carry):
            at = pl.multiple_of(j * tile_k, tile_k)
            keys = pl.ds(at, tile_k)
            allowed = allowed_tile(start_row, at, i * tile_q, tile_k, tile_q)
            result = []
            for h in range(heads):
                scores = jnp.dot(k_ref[h, keys], qt_ref[h, :, span], preferred_element_type=f32)
                grad_probs = jnp.dot(
                    v_ref[h, keys], grad_ref[h, :, span], preferred_element_type=f32
                )
                probs = jnp.exp(
                    jnp.where(allowed, scores * scale, MASK_FILL) - total_ref[h, :, span]
                )
                dv_sum[h, keys] += jnp.dot(
                    probs.astype(bf16), grad_rows[h, span], preferred_element_type=f32
                )
                grad_scores = (scale * probs * (grad_probs - delta[h, :, span])).astype(bf16)
                dk_sum[h, keys] += jnp.dot(
                    grad_scores, q_ref[h, span], preferred_element_type=f32
                )
                result.append(
                    carry[h]
                    + jnp.dot(kt_ref[h, :, keys], grad_scores, preferred_element_type=f32)
                )
            return tuple(result)

        done = lax.fori_loop(
            0, (i + 1) * tile_q // tile_k, step, (jnp.zeros((HD, tile_q), f32),) * heads
        )
        for h in range(heads):
            dq_sum[h, :, span] = done[h]
        if i == blocks // 2:
            up_sum[...] = finish_stage(
                up_ref[:, f], views[0], up_got, 0, f, fsdp, *one
            ).astype(bf16)
        if i == max(blocks // 2 - 1, 0):
            sends += start_spread(up_sum, up_out, 0, s, sp, *two)
            up_out[s] = up_sum[s]
    down_sum[...] = finish_stage(
        down_ref[f], views[1], down_got, 1, f, fsdp, *one
    ).astype(bf16)
    dense_out[...] = finish_stage(dense_ref[f], views[2], dense_got, 2, f, fsdp, *one)
    move = remote(
        down_sum, down_out, move_send, move_recv, sp=spot // fsdp, fsdp=spot % fsdp
    )
    keep = pltpu.make_async_copy(down_sum, down_out, own_sem)

    @pl.when(spot != rank)
    def _():
        move.start()

    @pl.when(spot == rank)
    def _():
        keep.start()

    half = ROT // 2
    cosine, sine = cos_ref[...], sin_ref[...]
    for h in range(heads):
        base = h * 3 * HD
        parts = (dq_sum[h], dk_sum[h].T, dv_sum[h].T)
        for j, part in enumerate(parts):
            part = part.astype(bf16).astype(f32)
            if j < 2:
                low, high = part[:half], part[half : 2 * half]
                part = jnp.concatenate(
                    [low * cosine + high * sine, high * cosine - low * sine, part[2 * half :]],
                    axis=0,
                )
            rows = pl.ds(base + j * HD, HD)
            joined_out[rows] = part.astype(bf16)
            bias_out[rows] = jnp.sum(part, axis=1, keepdims=True)
    finish_spread(up_sum, up_out, 0, s, sp, *two)

    @pl.when(spot != rank)
    def _():
        move.wait()

    @pl.when(spot == rank)
    def _():
        keep.wait()

    for copy in sends:
        copy.wait_send()


def attend_backward(grad_up, grad_down, grad_dense, start_row, q, k, v, qt, kt, grad_t, exact, total, cosine, sine):
    f32, bf16 = jnp.float32, jnp.bfloat16
    heads, length, head_dim = k.shape
    shape = jax.ShapeDtypeStruct
    cols = heads * 3 * head_dim
    pairs = heads * length * length // 2
    sp, fsdp = lax.axis_size("sp"), lax.axis_size("fsdp")
    up = (sp,) + grad_up.shape[2:]
    down, dense = grad_down.shape[1:], grad_dense.shape[1:]
    dma = pltpu.SemaphoreType.DMA
    return pl.pallas_call(
        functools.partial(
            attend_back_kernel, heads, min(512, length), min(256, length),
            1.0 / math.sqrt(head_dim), sp, fsdp,
        ),
        out_shape=[
            shape((cols, length), bf16), shape((cols, 1), f32),
            shape(up, bf16), shape(down, bf16), shape(dense, f32),
        ],
        in_specs=[pl.BlockSpec(memory_space=pltpu.VMEM)] * 14,
        out_specs=[pl.BlockSpec(memory_space=pltpu.VMEM)] * 5,
        scratch_shapes=[
            pltpu.VMEM((heads, length, head_dim), bf16),
            pltpu.VMEM((heads, 1, length), f32),
            pltpu.VMEM((heads, head_dim, length), f32),
            pltpu.VMEM((heads, length, head_dim), f32),
            pltpu.VMEM((heads, length, head_dim), f32),
            pltpu.VMEM((fsdp,) + up, bf16), pltpu.VMEM((fsdp,) + down, bf16),
            pltpu.VMEM((fsdp,) + dense, bf16),
            pltpu.VMEM(up, bf16), pltpu.VMEM(down, bf16),
            dma((3, fsdp)), dma((3, fsdp)), dma((1, sp)), dma((1, sp)), dma, dma, dma,
        ],
        compiler_params=pltpu.CompilerParams(
            collective_id=3, has_side_effects=True, vmem_limit_bytes=48 << 20
        ),
        cost_estimate=pl.CostEstimate(
            flops=40 * pairs * head_dim, transcendentals=pairs, bytes_accessed=24 * k.size
        ),
        name="attend_back",
    )(
        grad_up, grad_down, grad_dense, start_row, q, k, v, qt, kt, grad_t, exact, total,
        cosine, sine,
    )


MESH = pl.DeviceIdType.MESH


def remote(src, dst, send_sem, recv_sem, **target):
    return pltpu.make_async_remote_copy(
        src_ref=src, dst_ref=dst, send_sem=send_sem, recv_sem=recv_sem,
        device_id=target, device_id_type=MESH,
    )


def entry_barrier(targets):
    barrier = pltpu.get_barrier_semaphore()
    for target in targets:
        pl.semaphore_signal(barrier, inc=1, device_id=target, device_id_type=MESH)
    pl.semaphore_wait(barrier, len(targets))


def gather_kernel(
    sp, fsdp,
    x_ref, pos_ref, qkv_ref, up_ref, down_ref, dense_ref, *rest,
):
    count = (len(rest) - 13) // 2
    vec_refs, rest = rest[:count], rest[count:]
    x_out, pos_out, qkv_out, up_out, down_out, dense_out, *rest = rest
    vec_outs, rest = rest[:count], rest[count:]
    own_sem, line_send, x_recv, pos_send, pos_recv, w_send, w_recv = rest
    s, f = lax.axis_index("sp"), lax.axis_index("fsdp")
    chips = sp // 2
    chip, core = s // 2, s % 2
    partner = chip * 2 + (1 - core)
    head_rows = dense_out.shape[0]
    ff_piece = down_out.shape[1]
    dense_owner = s // (sp // fsdp)
    dense_part = s % (sp // fsdp)
    dense_src = dense_ref.at[pl.ds(pl.multiple_of(dense_part * head_rows, head_rows), head_rows)]
    down_src = down_ref.at[pl.ds(pl.multiple_of(s * ff_piece, ff_piece), ff_piece)]
    has_right, has_left = chip < chips - 1, chip > 0

    entry_barrier(
        [{"sp": (s + d) % sp} for d in range(1, sp)]
        + [{"fsdp": (f + d) % fsdp} for d in range(1, fsdp)]
    )

    def x_copy(src, block, sem, target):
        return remote(src, x_out.at[block], sem, x_recv.at[block], sp=target)

    def on(cond, copy, action):
        @pl.when(cond)
        def _():
            getattr(copy, action)()

    right = [x_copy(x_ref, s, line_send.at[0, 0], s + 2)]
    left = [x_copy(x_ref, s, line_send.at[1, 0], s - 2)]
    across_left = [x_copy(x_ref, s, line_send.at[2, 0], partner)]
    across_right = [None]
    on(has_right, right[0], "start")
    on(has_left, left[0], "start")
    across_left[0].start()

    def place(out, slot, cols):
        return out.at[slot] if cols is None else out.at[slot, :, cols]

    qkv_cols = qkv_out.shape[2]
    qkv_src = qkv_ref
    if qkv_ref.shape[1] != qkv_cols:
        qkv_src = qkv_ref.at[:, pl.ds(pl.multiple_of(s * qkv_cols, qkv_cols), qkv_cols)]
    pieces = [(qkv_src, qkv_out, None)]
    pieces += [(src, out, None) for src, out in zip(vec_refs, vec_outs)]
    first = len(pieces)
    pieces.append((down_src, down_out, None))
    if up_ref.shape[1] != up_out.shape[2]:
        for c in range(fsdp):
            at = pl.multiple_of((c * sp + s) * ff_piece, ff_piece)
            pieces.append(
                (up_ref.at[:, pl.ds(at, ff_piece)], up_out, pl.ds(c * ff_piece, ff_piece))
            )
    else:
        pieces.append((up_ref, up_out, None))
    dense_slot = len(pieces)
    sends = []
    for d in range(1, fsdp):
        peer = (f + d) % fsdp
        for k, (src, out, cols) in enumerate(pieces[:first]):
            sends.append(
                remote(src, place(out, f, cols), w_send.at[k, d], w_recv.at[k, f], fsdp=peer)
            )
    dense_sends = [
        remote(dense_src, dense_out, w_send.at[dense_slot, d], w_recv.at[dense_slot, 0],
               fsdp=(f + d) % fsdp)
        for d in range(1, fsdp)
    ]
    for d in range(1, fsdp):
        peer = (f + d) % fsdp
        for k, (src, out, cols) in enumerate(pieces[first:], first):
            sends.append(
                remote(src, place(out, f, cols), w_send.at[k, d], w_recv.at[k, f], fsdp=peer)
            )
    for copy in sends[: first * (fsdp - 1)]:
        copy.start()
    is_owner = f == dense_owner
    for copy in dense_sends:
        on(is_owner, copy, "start")
    for copy in sends[first * (fsdp - 1) :]:
        copy.start()
    pos_sends = []
    for d in range(1, sp):
        peer = (s + d) % sp
        pos_sends.append(remote(pos_ref, pos_out.at[s], pos_send.at[d], pos_recv.at[s], sp=peer))
        pos_sends[-1].start()
    own = [
        pltpu.make_async_copy(src, place(out, f, cols), own_sem.at[k])
        for k, (src, out, cols) in enumerate(pieces)
    ]
    own_dense = pltpu.make_async_copy(dense_src, dense_out, own_sem.at[dense_slot])
    own.append(pltpu.make_async_copy(x_ref, x_out.at[s], own_sem.at[dense_slot + 1]))
    own.append(pltpu.make_async_copy(pos_ref, pos_out.at[s], own_sem.at[dense_slot + 2]))
    for copy in own:
        copy.start()
    on(is_owner, own_dense, "start")

    for k in range(1, chips):
        from_left, from_right = s - 2 * k, s + 2 * k
        has_l, has_r = chip >= k, chip + k <= chips - 1
        held_l, held_r = x_out.at[from_left], x_out.at[from_right]
        right.append(x_copy(held_l, from_left, line_send.at[0, k], s + 2))
        left.append(x_copy(held_r, from_right, line_send.at[1, k], s - 2))
        across_left.append(x_copy(held_l, from_left, line_send.at[2, k], partner))
        across_right.append(x_copy(held_r, from_right, line_send.at[3, k], partner))

        @pl.when(has_l)
        def _():
            across_left[k].wait_recv()

            @pl.when(has_right)
            def _():
                right[k].start()

            across_left[k].start()

        @pl.when(has_r)
        def _():
            across_right[k].wait_recv()

            @pl.when(has_left)
            def _():
                left[k].start()

            across_right[k].start()

    for c in range(chips):
        block = 2 * c + (1 - core)
        x_copy(x_ref, block, line_send.at[0, 0], partner).wait_recv()
    for d in range(1, sp):
        block = (s + d) % sp
        remote(pos_ref, pos_out.at[block], pos_send.at[0], pos_recv.at[block], sp=block).wait_recv()
    for d in range(1, fsdp):
        peer = (f + d) % fsdp
        for k, (src, out, cols) in enumerate(pieces):
            remote(
                src, place(out, peer, cols), w_send.at[k, 0], w_recv.at[k, peer], fsdp=peer
            ).wait_recv()
    not_owner = f != dense_owner
    on(not_owner, dense_sends[0], "wait_recv")
    for copy in own:
        copy.wait()
    on(is_owner, own_dense, "wait")
    for copy in sends + pos_sends:
        copy.wait_send()
    for copy in dense_sends:
        on(is_owner, copy, "wait_send")
    on(has_right, right[0], "wait_send")
    on(has_left, left[0], "wait_send")
    across_left[0].wait_send()
    for k in range(1, chips):
        has_l, has_r = chip >= k, chip + k <= chips - 1

        @pl.when(has_l)
        def _():
            across_left[k].wait_send()

            @pl.when(has_right)
            def _():
                right[k].wait_send()

        @pl.when(has_r)
        def _():
            across_right[k].wait_send()

            @pl.when(has_left)
            def _():
                left[k].wait_send()


def gather_all(
    hidden, positions, vectors, qkv_own, up_own, down_weight, dense_weight, qkv_cols, ff_piece
):
    sp, fsdp = lax.axis_size("sp"), lax.axis_size("fsdp")
    bf16 = jnp.bfloat16
    width = down_weight.shape[1]
    shapes = (
        ((sp,) + hidden.shape, bf16),
        ((sp,) + positions.shape, jnp.int32),
        ((fsdp, qkv_own.shape[0], qkv_cols), bf16),
        ((fsdp, up_own.shape[0], ff_piece * fsdp), bf16),
        ((fsdp, ff_piece, width), bf16),
        ((width // sp, width), bf16),
    ) + tuple(((fsdp,) + vector.shape, bf16) for vector in vectors)
    count = len(vectors)
    dma = pltpu.SemaphoreType.DMA
    return pl.pallas_call(
        functools.partial(gather_kernel, sp, fsdp),
        out_shape=[jax.ShapeDtypeStruct(*shape) for shape in shapes],
        in_specs=[pl.BlockSpec(memory_space=pltpu.HBM)] * (6 + count),
        out_specs=[pl.BlockSpec(memory_space=pltpu.VMEM)] * (6 + count),
        scratch_shapes=[
            dma((fsdp + count + 5,)), dma((4, sp // 2)), dma((sp,)), dma((sp,)), dma((sp,)),
            dma((fsdp + count + 3, fsdp)), dma((fsdp + count + 3, fsdp)),
        ],
        compiler_params=pltpu.CompilerParams(
            collective_id=1, has_side_effects=True, vmem_limit_bytes=40 << 20
        ),
        name="gather_all",
    )(hidden, positions, qkv_own, up_own, down_weight, dense_weight, *vectors)


def start_stage(views, gots, f, fsdp, send, recv):
    sends = []
    for k, (view, got) in enumerate(zip(views, gots)):
        for d in range(1, fsdp):
            peer = (f + d) % fsdp
            sends.append(remote(view(peer), got.at[f], send.at[k, d], recv.at[k, f], fsdp=peer))
            sends[-1].start()
    return sends


def finish_stage(own, view, got, k, f, fsdp, send, recv):
    for d in range(1, fsdp):
        peer = (f + d) % fsdp
        remote(view(peer), got.at[peer], send.at[k, 0], recv.at[k, peer], fsdp=peer).wait_recv()
    total = own.astype(jnp.float32)
    for d in range(1, fsdp):
        total = total + got[(f + d) % fsdp].astype(jnp.float32)
    return total


def start_spread(source, out, k, s, sp, send, recv):
    copies = []
    for d in range(1, sp):
        peer = (s + d) % sp
        copies.append(
            remote(source.at[peer], out.at[s], send.at[k, d], recv.at[k, s], sp=peer)
        )
        copies[-1].start()
    return copies


def finish_spread(source, out, k, s, sp, send, recv):
    for d in range(1, sp):
        peer = (s + d) % sp
        remote(
            source.at[peer], out.at[peer], send.at[k, 0], recv.at[k, peer], sp=peer
        ).wait_recv()


def reduce_kernel(
    sp, fsdp, qkv_ref, vec_ref, qkv_out, vec_out,
    qkv_got, vec_got, qkv_sum, vec_sum, vec_two, send_one, recv_one, send_two, recv_two,
):
    bf16 = jnp.bfloat16
    s, f = lax.axis_index("sp"), lax.axis_index("fsdp")
    entry_barrier(
        [{"sp": (s + d) % sp} for d in range(1, sp)]
        + [{"fsdp": (f + d) % fsdp} for d in range(1, fsdp)]
    )
    views = [lambda j: vec_ref.at[:, j], lambda j: qkv_ref.at[:, j]]
    gots = [vec_got, qkv_got]
    one, two = (send_one, recv_one), (send_two, recv_two)
    sends = start_stage(views, gots, f, fsdp, *one)
    vec_sum[...] = finish_stage(vec_ref[:, f], views[0], vec_got, 0, f, fsdp, *one)
    qkv_sum[...] = finish_stage(qkv_ref[:, f], views[1], qkv_got, 1, f, fsdp, *one).astype(bf16)
    sends += start_spread(vec_sum, vec_two, 0, s, sp, *two)
    vec_two[s] = vec_sum[s]
    qkv_out[s] = qkv_sum[s]
    sends += start_spread(qkv_sum, qkv_out, 1, s, sp, *two)
    finish_spread(vec_sum, vec_two, 0, s, sp, *two)
    total = vec_two[0]
    for j in range(1, sp):
        total = total + vec_two[j]
    vec_out[...] = total
    finish_spread(qkv_sum, qkv_out, 1, s, sp, *two)
    for copy in sends:
        copy.wait_send()


def reduce_all(grad_qkv, vectors):
    sp, fsdp = lax.axis_size("sp"), lax.axis_size("fsdp")
    f32, bf16 = jnp.float32, jnp.bfloat16
    qkv, vec = ((sp,) + grad.shape[2:] for grad in (grad_qkv, vectors))
    dma = pltpu.SemaphoreType.DMA
    return pl.pallas_call(
        functools.partial(reduce_kernel, sp, fsdp),
        out_shape=[jax.ShapeDtypeStruct(qkv, bf16), jax.ShapeDtypeStruct(vec[1:], f32)],
        in_specs=[pl.BlockSpec(memory_space=pltpu.VMEM)] * 2,
        out_specs=[pl.BlockSpec(memory_space=pltpu.VMEM)] * 2,
        scratch_shapes=[
            pltpu.VMEM((fsdp,) + qkv, bf16), pltpu.VMEM((fsdp,) + vec, f32),
            pltpu.VMEM(qkv, bf16), pltpu.VMEM(vec, f32), pltpu.VMEM(vec, f32),
            dma((2, fsdp)), dma((2, fsdp)), dma((2, sp)), dma((2, sp)),
        ],
        compiler_params=pltpu.CompilerParams(
            collective_id=2, has_side_effects=True, vmem_limit_bytes=40 << 20
        ),
        cost_estimate=pl.CostEstimate(
            flops=0, transcendentals=0, bytes_accessed=100_000_000
        ),
        name="reduce_all",
    )(grad_qkv, vectors)


def local(
    hidden_in,
    positions,
    out_cotangent,
    attn_gain,
    attn_shift,
    mlp_gain,
    mlp_shift,
    qkv_weight,
    qkv_bias,
    dense_weight,
    dense_bias,
    up_weight,
    up_bias,
    down_weight,
    down_bias,
):
    f32, bf16 = jnp.float32, jnp.bfloat16
    seq_count, local_len, width = hidden_in.shape
    sp_size, fsdp_size = lax.axis_size("sp"), lax.axis_size("fsdp")
    sp_index = lax.axis_index("sp")
    total_len = local_len * sp_size
    rows_all = seq_count * total_len
    own_width = width // fsdp_size
    heads_here = HEADS // sp_size
    qkv_cols = qkv_weight.shape[1] // sp_size
    head_cols = width // sp_size
    ff_all = up_weight.shape[1]
    ff_piece = ff_all // (sp_size * fsdp_size)
    ff_here = ff_piece * fsdp_size
    own_rows = width // (sp_size * fsdp_size)

    qkv_own, up_own = qkv_weight, up_weight
    if qkv_cols % 128:
        qkv_own = lax.dynamic_slice_in_dim(qkv_weight, sp_index * qkv_cols, qkv_cols, axis=1)
    if ff_piece % 128:
        up_own = lax.dynamic_slice_in_dim(
            up_weight.reshape(own_width, fsdp_size, sp_size, ff_piece), sp_index, 1, axis=2
        ).reshape(own_width, ff_here)
    vectors = [
        vector[None]
        for vector in (
            attn_gain, attn_shift, mlp_gain, mlp_shift, dense_bias, down_bias, qkv_bias, up_bias
        )
    ]
    x_all, all_positions, w_qkv, w_up, w_down, w_dense, *vectors = gather_all(
        hidden_in,
        positions,
        vectors,
        qkv_own,
        up_own,
        down_weight,
        dense_weight,
        qkv_cols,
        ff_piece,
    )
    cot_own, x_all = lax.optimization_barrier((out_cotangent, x_all))
    cot_all = lax.all_gather(cot_own, "sp", axis=1, tiled=True)
    x_all = x_all.transpose(1, 0, 2, 3).reshape(seq_count, total_len, width)
    all_positions = all_positions.transpose(1, 0, 2).reshape(seq_count, total_len)
    w_qkv = w_qkv.reshape(width, qkv_cols)
    w_up = w_up.reshape(width, ff_here)
    w_down = w_down.reshape(ff_here, width)
    *vectors, b_up = vectors
    g_attn, s_attn, g_mlp, s_mlp, b_dense, b_down, b_qkv = (v.reshape(-1) for v in vectors)
    b_qkv = lax.dynamic_slice_in_dim(b_qkv, sp_index * qkv_cols, qkv_cols)
    b_up = lax.dynamic_slice_in_dim(
        b_up.reshape(fsdp_size, -1), sp_index * ff_piece, ff_piece, axis=1
    ).reshape(ff_here)

    cot_rows = cot_all.reshape(rows_all, width)
    flat_positions = all_positions.reshape(rows_all)
    cosine, sine = rope_rows(flat_positions, ROT)
    start_row = (jnp.arange(rows_all, dtype=jnp.int32) - flat_positions)[None]
    affine_rows = jnp.stack([g_attn, s_attn, g_mlp, s_mlp]).astype(f32)
    x_rows = x_all.reshape(rows_all, width)
    attn_in, mlp_in, row_mean, row_inv, q, k, v, qt, kt, vt = project(
        x_rows, w_qkv, b_qkv.astype(f32)[None], affine_rows, cosine, sine, heads_here
    )
    mixed_t, exact, log_total = attend_forward(start_row, k, qt, vt)
    mixed_t = mixed_t.reshape(head_cols, rows_all)
    up_out = jnp.dot(mlp_in, w_up, preferred_element_type=f32) + b_up.astype(f32)
    activated, gelu_slope = gelu_pair(up_out)
    activated = activated.astype(bf16)
    out_part = jnp.einsum("dr,de->re", mixed_t, w_dense, preferred_element_type=f32) + jnp.dot(
        activated, w_down, preferred_element_type=f32
    )
    out_part, cot_rows = lax.optimization_barrier((out_part.astype(bf16), cot_rows))
    out_sum = lax.psum_scatter(
        out_part.reshape(seq_count, total_len, width),
        "sp", scatter_dimension=1, tiled=True,
    )

    grad_up = jnp.einsum("rd,fd->rf", cot_rows, w_down, preferred_element_type=f32) * gelu_slope
    grad_up_half = grad_up.astype(bf16)
    up_bias_part = jnp.sum(grad_up, axis=0)
    grad_mlp_in = jnp.einsum("rf,df->rd", grad_up_half, w_up, preferred_element_type=f32)
    grad_heads = (
        jnp.einsum("de,re->dr", w_dense, cot_rows, preferred_element_type=f32)
        .astype(bf16)
        .reshape(heads_here, HD, rows_all)
    )
    grad_down = jnp.einsum("rf,rd->fd", activated, cot_rows, preferred_element_type=f32)
    grad_dense = jnp.einsum("dr,re->de", mixed_t, cot_rows, preferred_element_type=f32)
    grad_up_weight = jnp.einsum("rd,rf->df", mlp_in, grad_up_half, preferred_element_type=f32)
    own_sum = jnp.sum(out_cotangent.astype(f32), axis=(0, 1))
    grad_down, grad_dense, grad_up_weight, grad_heads, own_sum = lax.optimization_barrier(
        (
            grad_down.astype(bf16), grad_dense.astype(bf16), grad_up_weight.astype(bf16),
            grad_heads, own_sum,
        )
    )
    joined_half, qkv_bias_part, up_rows, down_rows, dense_grad = attend_backward(
        grad_up_weight.reshape(sp_size, fsdp_size, own_rows, ff_here),
        grad_down.reshape(fsdp_size, ff_piece, width),
        grad_dense.reshape(fsdp_size, own_rows, width),
        start_row, q, k, v, qt, kt, grad_heads, exact, log_total, cosine, sine
    )
    qkv_bias_part = qkv_bias_part.reshape(qkv_cols)

    grad_attn_in = jnp.einsum("cr,dc->rd", joined_half, w_qkv, preferred_element_type=f32)
    normed_part = grad_attn_in * g_attn.astype(f32) + grad_mlp_in * g_mlp.astype(f32)
    normed_part, joined_half, out_sum = lax.optimization_barrier(
        (normed_part.astype(bf16), joined_half, out_sum)
    )
    grad_normed = lax.psum_scatter(
        normed_part.reshape(seq_count, total_len, width),
        "sp", scatter_dimension=1, tiled=True,
    ).astype(f32)
    grad_qkv = jnp.einsum(
        "rd,cr->dc", attn_in, joined_half, preferred_element_type=f32
    ).astype(bf16)

    x_own = hidden_in.astype(f32)
    block_out = (
        x_own + out_sum.astype(f32) + (b_dense.astype(f32) + b_down.astype(f32))
    ).astype(bf16)

    owners = sp_size * fsdp_size
    up_bias_full = lax.dynamic_update_slice_in_dim(
        jnp.zeros((fsdp_size, sp_size, ff_piece), f32),
        up_bias_part.reshape(fsdp_size, 1, ff_piece), sp_index, axis=1,
    ).reshape(owners, ff_piece)
    qkv_bias_full = lax.dynamic_update_slice_in_dim(
        jnp.zeros((sp_size * qkv_cols,), f32), qkv_bias_part, sp_index * qkv_cols, axis=0
    ).reshape(owners, -1)
    grad_own = out_cotangent.astype(f32)
    normed_all = (x_rows.astype(f32) - row_mean) * row_inv
    sums = [
        jnp.sum(grad_attn_in * normed_all, axis=0),
        jnp.sum(grad_attn_in, axis=0),
        jnp.sum(grad_mlp_in * normed_all, axis=0),
        jnp.sum(grad_mlp_in, axis=0),
        own_sum,
    ]
    vector_parts = jnp.concatenate(
        [up_bias_full, qkv_bias_full] + [v.reshape(owners, own_rows) for v in sums], axis=1
    )
    qkv_rows, vector_sums = reduce_all(
        grad_qkv.reshape(sp_size, fsdp_size, own_rows, qkv_cols),
        vector_parts.reshape(sp_size, fsdp_size, 1, -1),
    )
    down_grad = down_rows.astype(f32)
    up_grad = (
        up_rows.reshape(sp_size, own_rows, fsdp_size, ff_piece)
        .transpose(1, 2, 0, 3)
        .reshape(own_rows, ff_all)
        .astype(f32)
    )
    qkv_grad = (
        qkv_rows.transpose(1, 0, 2).reshape(own_rows, sp_size * qkv_cols).astype(f32)
    )
    vector_sums = vector_sums[0]
    qkv_piece = qkv_cols // fsdp_size
    up_bias_grad = vector_sums[:ff_piece]
    qkv_bias_grad = vector_sums[ff_piece : ff_piece + qkv_piece]
    tail = vector_sums[ff_piece + qkv_piece :]
    attn_gain_grad, attn_shift_grad, mlp_gain_grad, mlp_shift_grad, output_bias_grad = (
        tail[k * own_rows : (k + 1) * own_rows] for k in range(5)
    )

    normed_own, inv_std = layer_norm(x_own)
    mean_grad = jnp.mean(grad_normed, axis=-1, keepdims=True)
    mean_cross = jnp.mean(grad_normed * normed_own, axis=-1, keepdims=True)
    input_grad = grad_own + inv_std * (grad_normed - mean_grad - normed_own * mean_cross)
    return (
        block_out,
        input_grad,
        attn_gain_grad,
        attn_shift_grad,
        mlp_gain_grad,
        mlp_shift_grad,
        qkv_grad,
        qkv_bias_grad,
        dense_grad,
        output_bias_grad,
        up_grad,
        up_bias_grad,
        down_grad,
        output_bias_grad,
    )


def solution(mesh):
    placed = (
        P("fsdp", "sp", None),
        P("fsdp", "sp"),
        P("fsdp", "sp", None),
        P("fsdp"),
        P("fsdp"),
        P("fsdp"),
        P("fsdp"),
        P("fsdp", None),
        P("fsdp"),
        P("fsdp", None),
        P("fsdp"),
        P("fsdp", None),
        P("fsdp"),
        P("fsdp", None),
        P("fsdp"),
    )
    return jax.shard_map(
        local,
        mesh=mesh,
        in_specs=placed,
        out_specs=(
            P("fsdp", "sp", None),
            P("fsdp", "sp", None),
            P(("sp", "fsdp")),
            P(("sp", "fsdp")),
            P(("sp", "fsdp")),
            P(("sp", "fsdp")),
            P(("sp", "fsdp"), None),
            P(("sp", "fsdp")),
            P(("sp", "fsdp"), None),
            P(("sp", "fsdp")),
            P(("sp", "fsdp"), None),
            P(("sp", "fsdp")),
            P(("sp", "fsdp"), None),
            P(("sp", "fsdp")),
        ),
        check_vma=False,
    )
```
